32 devices in a mesh: dp: 8 (over z, y), fsdp: 4 (over x, core).
Axes of the slice: x: 2, y: 2, z: 4, core: 2. Of those that a mesh axis runs over, the one named last changes fastest.
Arguments:
- tokens: bfloat16 [64, 1024, 768], P(('dp', 'fsdp')), may hold values from -6 to 6
- seg_ids: int32 [64, 1024], P(('dp', 'fsdp')), may hold values from 0 to 17, as said below
- pad_mask: int32 [64, 1024], P(('dp', 'fsdp')), may hold values from 0 to 1, as said below
- w_query: bfloat16 [768, 768], P(('dp', 'fsdp')), may hold values from -0.625 to 0.625
- w_key: bfloat16 [768, 768], P(('dp', 'fsdp')), may hold values from -0.625 to 0.625
- w_value: bfloat16 [768, 768], P(('dp', 'fsdp')), may hold values from -0.21875 to 0.21875
- w_out: bfloat16 [768, 768], P(('dp', 'fsdp')), may hold values from -0.625 to 0.625
- w_in: bfloat16 [768, 3072], P(('dp', 'fsdp')), may hold values from -0.21875 to 0.21875
- w_back: bfloat16 [3072, 768], P(('dp', 'fsdp')), may hold values from -0.109375 to 0.109375
- b_query: bfloat16 [768], P(('dp', 'fsdp')), may hold values from -6 to 6
- b_value: bfloat16 [768], P(('dp', 'fsdp')), may hold values from -3 to 3
- b_out: bfloat16 [768], P(('dp', 'fsdp')), may hold values from -1.75 to 1.75
- gain_attn: bfloat16 [768], P(('dp', 'fsdp')), may hold values from 0.5 to 1.5
- shift_attn: bfloat16 [768], P(('dp', 'fsdp')), may hold values from -1.75 to 1.75
- b_in: bfloat16 [3072], P(('dp', 'fsdp')), may hold values from -3 to 3
- b_back: bfloat16 [768], P(('dp', 'fsdp')), may hold values from -1.75 to 1.75
- gain_ffn: bfloat16 [768], P(('dp', 'fsdp')), may hold values from 0.5 to 1.5
- shift_ffn: bfloat16 [768], P(('dp', 'fsdp')), may hold values from -1.75 to 1.75
- conv_weight: bfloat16 [12, 33], replicated, may hold values from -0.375 to 0.375
- cotangent: bfloat16 [64, 1024, 768], P(('dp', 'fsdp')), may hold values from -6 to 6
Outputs:
- output: bfloat16 [64, 1024, 768], P(('dp', 'fsdp'))
- grad_tokens: bfloat16 [64, 1024, 768], P(('dp', 'fsdp'))
- grad_w_query: float32 [768, 768], P(('dp', 'fsdp'))
- grad_w_key: float32 [768, 768], P(('dp', 'fsdp'))
- grad_w_value: float32 [768, 768], P(('dp', 'fsdp'))
- grad_w_out: float32 [768, 768], P(('dp', 'fsdp'))
- grad_w_in: float32 [768, 3072], P(('dp', 'fsdp'))
- grad_w_back: float32 [3072, 768], P(('dp', 'fsdp'))
- grad_b_query: float32 [768], P(('dp', 'fsdp'))
- grad_b_value: float32 [768], P(('dp', 'fsdp'))
- grad_b_out: float32 [768], P(('dp', 'fsdp'))
- grad_gain_attn: float32 [768], P(('dp', 'fsdp'))
- grad_shift_attn: float32 [768], P(('dp', 'fsdp'))
- grad_b_in: float32 [3072], P(('dp', 'fsdp'))
- grad_b_back: float32 [768], P(('dp', 'fsdp'))
- grad_gain_ffn: float32 [768], P(('dp', 'fsdp'))
- grad_shift_ffn: float32 [768], P(('dp', 'fsdp'))
- grad_conv: float32 [12, 33], replicated
The draws below stay inside these ranges and needn't reach their ends.
Inputs may be any that keep to these rules, and one draw needn't show every extreme that they name: `seg_ids`: within a sequence the live tokens form whole documents of 60 to 800 tokens numbered 0, 1, 2 and so on in order; every padding token carries the number 1024 // 60. `pad_mask`: 1 on each sequence's tokens up to the end of its last whole document, 0 after; the last token of every sequence is padding.
All inputs are finite; a program needn't handle non-finite values.
Results may differ from the reference program's by a relative error of at most 0.025.
The reference program's roundings to bfloat16 on the way count: a program that leaves them out, or rounds other values in their place, can miss the bound.
Values may be sent and summed in bfloat16 or wider, within the bound.
A program may use at most 384 MiB of HBM per device.

```python
import jax
import jax.numpy as jnp
from jax import lax

D = 768
HEADS = 12
FF = 3072
LAND = 64
KCONV = 33
PINV_STEPS = 6
SEQ_LEN = 1024
DOC_MIN = 60
DOC_MAX = 800
SEQS = 64


def doc_layout(key):
    doc_slots = SEQ_LEN // DOC_MIN + 1
    doc_lengths = jax.random.randint(jax.random.fold_in(key, 11), (SEQS, doc_slots), DOC_MIN, DOC_MAX + 1)
    doc_ends = jnp.cumsum(doc_lengths, axis=1)
    fitting = doc_ends <= SEQ_LEN - 1
    live_length = jnp.max(jnp.where(fitting, doc_ends, 0), axis=1)
    positions = jnp.arange(SEQ_LEN, dtype=jnp.int32)
    segments = jnp.sum((doc_ends[:, None, :] <= positions[None, :, None]).astype(jnp.int32), axis=2)
    padding = (positions[None, :] < live_length[:, None]).astype(jnp.int32)
    segments = jnp.where(padding == 1, segments, SEQ_LEN // DOC_MIN)
    return (segments.astype(jnp.int32), padding)


def draw_seg_ids(key, part):
    return doc_layout(key)[0]


def draw_pad_mask(key, part):
    return doc_layout(key)[1]


def levels(key, extent, cuts, low, largest):
    def one(position, blocks):
        draws = jax.random.uniform(jax.random.fold_in(jax.random.fold_in(key, 6), position), (blocks,), jnp.float32, low / len(cuts), largest / len(cuts))
        return jnp.repeat(jnp.exp(draws), extent[position] // blocks).reshape((-1,) + (1,) * (len(extent) - position - 1))

    loudness = one(*cuts[0])
    for cut in cuts[1:]:
        loudness = loudness * one(*cut)
    return loudness


def centred(rng, dims, deviation, most, pieces=(), kind=jnp.bfloat16):
    array = jax.random.normal(rng, dims, jnp.float32) * deviation
    if len(pieces) > 0:
        array = levels(rng, dims, pieces, -0.22, 0.18) * array
    return jnp.clip(array, min=-most, max=most).astype(kind)


def setup_inputs(seed: int = 0) -> dict:
    key_of = jax.random.split(jax.random.key(seed), 21)
    return {
        "tokens": centred(key_of[0], (SEQS, SEQ_LEN, D), 1.0, 6.0, ((0, 32),)),
        "seg_ids": draw_seg_ids(jax.random.fold_in(key_of[20], 71), 0),
        "pad_mask": draw_pad_mask(jax.random.fold_in(key_of[20], 71), 0),
        "w_query": centred(key_of[3], (D, D), (D // 9) ** -0.5, 0.625, ((0, 32),)),
        "w_key": centred(key_of[4], (D, D), (D // 9) ** -0.5, 0.625, ((0, 32),)),
        "w_value": centred(key_of[5], (D, D), D ** -0.5, 0.21875, ((0, 32),)),
        "w_out": centred(key_of[6], (D, D), (D // 8) ** -0.5, 0.625, ((0, 32),)),
        "w_in": centred(key_of[7], (D, FF), D ** -0.5, 0.21875, ((0, 32),)),
        "w_back": centred(key_of[8], (FF, D), FF ** -0.5, 0.109375, ((0, 32),)),
        "b_query": centred(key_of[9], (D,), 1.0, 6.0, ((0, 32),)),
        "b_value": centred(key_of[10], (D,), 0.5, 3.0, ((0, 32),)),
        "b_out": centred(key_of[11], (D,), 0.3, 1.75, ((0, 32),)),
        "gain_attn": jnp.clip(1.0 + 0.1 * jax.random.normal(key_of[12], (D,), jnp.float32), 0.5, 1.5).astype(jnp.bfloat16),
        "shift_attn": centred(key_of[13], (D,), 0.3, 1.75, ((0, 32),)),
        "b_in": centred(key_of[14], (FF,), 0.5, 3.0, ((0, 32),)),
        "b_back": centred(key_of[15], (D,), 0.3, 1.75, ((0, 32),)),
        "gain_ffn": jnp.clip(1.0 + 0.1 * jax.random.normal(key_of[16], (D,), jnp.float32), 0.5, 1.5).astype(jnp.bfloat16),
        "shift_ffn": centred(key_of[17], (D,), 0.3, 1.75, ((0, 32),)),
        "conv_weight": centred(key_of[18], (HEADS, KCONV), 0.06, 0.375),
        "cotangent": centred(key_of[19], (SEQS, SEQ_LEN, D), 1.0, 6.0, ((0, 32),)),
    }


@jax.custom_vjp
def low(v):
    return lax.optimization_barrier(v.astype(jnp.bfloat16)).astype(jnp.float32)

@jax.custom_vjp
def low_back(v):
    return v

def low_keep(v):
    return (low(v), None)

def low_pass(kept, grad):
    return (grad,)

def back_keep(v):
    return (v, None)

def back_low(kept, grad):
    return (low(grad),)
low.defvjp(low_keep, low_pass)
low_back.defvjp(back_keep, back_low)
precise = lax.Precision.HIGHEST
neg_fill = -1e+30
norm_eps = 1e-05

def matmul_exact(left, right):
    return jnp.dot(left, right, precision=precise)

def contract(form, left, right):
    return jnp.einsum(form, left, right, precision=precise)

def shifted(array_in, offset, fill_value):
    if offset == 0:
        return array_in
    shift_width = abs(offset)
    filler = jnp.full((array_in.shape[0], shift_width) + array_in.shape[2:], fill_value, array_in.dtype)
    if offset > 0:
        return jnp.concatenate([array_in[:, offset:], filler], axis=1)
    return jnp.concatenate([filler, array_in[:, :offset]], axis=1)

def layouts(segments, padding, land_total):
    length = segments.shape[1]
    stride = length // land_total
    lead_seg = segments[:, ::stride]
    lead_live = padding[:, ::stride] == 1
    token_block = jnp.arange(length, dtype=jnp.int32) // stride
    land_index = jnp.arange(land_total, dtype=jnp.int32)
    same_doc = segments[:, None, :] == lead_seg[:, :, None]
    cross_mask = same_doc & (padding[:, None, :] == 1) & lead_live[:, :, None]
    member = cross_mask & (token_block[None, None, :] == land_index[None, :, None])
    among_mask = (lead_seg[:, :, None] == lead_seg[:, None, :]) & lead_live[:, :, None] & lead_live[:, None, :]
    land_count = jnp.maximum(lax.optimization_barrier(jnp.sum(member.astype(jnp.float32), axis=2)), 1.0)
    return (member.astype(jnp.float32), land_count, cross_mask, among_mask, lead_live.astype(jnp.float32))

def masked_softmax(scores, mask, axis):
    held_scores = jnp.where(mask, scores, neg_fill)
    row_top = lax.optimization_barrier(jnp.max(held_scores, axis=axis, keepdims=True))
    exp_terms = jnp.exp(held_scores - row_top)
    return exp_terms / lax.optimization_barrier(jnp.sum(exp_terms, axis=axis, keepdims=True))

def newton_pinv(matrix, step_count):
    order_size = matrix.shape[-1]
    identity = jnp.eye(order_size, dtype=matrix.dtype)
    frob_norm = lax.optimization_barrier(jnp.sum(matrix * matrix, axis=(-2, -1), keepdims=True)) + 1e-06
    inverse = jnp.swapaxes(matrix, -1, -2) / frob_norm
    for iteration in range(step_count):
        product = contract('...ij,...jk->...ik', matrix, inverse)
        bracket = 7.0 * identity - product
        bracket = 15.0 * identity - contract('...ij,...jk->...ik', product, bracket)
        bracket = 13.0 * identity - contract('...ij,...jk->...ik', product, bracket)
        inverse = 0.25 * contract('...ij,...jk->...ik', inverse, bracket)
    return inverse

def convolve(value_rows, kernel, segments, padding, head_dim):
    tap_count = kernel.shape[1]
    half_span = tap_count // 2
    total = jnp.zeros_like(value_rows)
    for tap_index in range(tap_count):
        offset = tap_index - half_span
        moved = shifted(value_rows, offset, 0.0)
        moved_seg = shifted(segments, offset, -1)
        moved_pad = shifted(padding, offset, 0)
        kept_mask = ((moved_seg == segments) & (moved_pad == 1)).astype(value_rows.dtype)
        weight = jnp.repeat(kernel[:, tap_index], head_dim)
        total = total + kept_mask[:, :, None] * weight[None, None, :] * moved
    return total

def layer_norm(resid, gain, shift):
    row_mean = lax.optimization_barrier(jnp.mean(resid, axis=-1, keepdims=True))
    centered = resid - row_mean
    variance = lax.optimization_barrier(jnp.mean(centered * centered, axis=-1, keepdims=True))
    return centered * lax.rsqrt(variance + norm_eps) * gain + shift

def block_forward(tokens, w_query, w_key, w_value, w_out, w_in, w_back, b_query, b_value, b_out, gain_attn, shift_attn, b_in, b_back, gain_ffn, shift_ffn, conv_weight, segments, padding):
    seq_count, length, model_width = tokens.shape
    head_count = conv_weight.shape[0]
    head_dim = model_width // head_count
    score_scale = head_dim ** (-0.5)
    member, land_count, cross_mask, among_mask, land_live = layouts(segments, padding, LAND)
    heads_shape = (seq_count, length, head_count, head_dim)
    flat_rows = tokens.reshape(seq_count * length, model_width)
    query_heads = low(low_back(matmul_exact(flat_rows, w_query) + b_query)).reshape(heads_shape)
    key_heads = low(low_back(matmul_exact(flat_rows, w_key))).reshape(heads_shape)
    value_heads = low(low_back(matmul_exact(flat_rows, w_value) + b_value)).reshape(heads_shape)
    land_query = low(contract('bjt,bthe->bjhe', member, query_heads) / land_count[:, :, None, None])
    land_key = low(contract('bjt,bthe->bjhe', member, key_heads) / land_count[:, :, None, None])
    score_f = contract('bjhe,bthe->bhjt', land_key, query_heads) * score_scale
    kern_f = low(masked_softmax(low_back(score_f), cross_mask[:, None], -2))
    score_b = contract('bjhe,bthe->bhjt', land_query, key_heads) * score_scale
    kern_b = low(masked_softmax(low_back(score_b), cross_mask[:, None], -1) * land_live[:, None, :, None])
    score_a = contract('bihe,bjhe->bhij', land_query, land_key) * score_scale
    kern_a = masked_softmax(low_back(score_a), among_mask[:, None], -1) * land_live[:, None, :, None]
    inverse = newton_pinv(kern_a, PINV_STEPS)
    summary = low_back(contract('bhjt,bthe->bhje', kern_b, value_heads))
    mixed_heads = low(contract('bhij,bhje->bhie', inverse, summary))
    approx = contract('bhjt,bhje->bthe', kern_f, mixed_heads).reshape(seq_count, length, model_width)
    local_conv = convolve(value_heads.reshape(seq_count, length, model_width), conv_weight, segments, padding, head_dim)
    attended = (approx + local_conv) * padding[:, :, None].astype(approx.dtype)
    attended = low(low_back(attended.reshape(seq_count * length, model_width)))
    branch = low_back(matmul_exact(attended, w_out) + b_out)
    hidden = layer_norm(flat_rows + branch, gain_attn, shift_attn)
    inner_act = low_back(matmul_exact(low(hidden), w_in) + b_in)
    active = low(jax.nn.gelu(inner_act, approximate=False))
    feed_out = low_back(matmul_exact(active, w_back) + b_back)
    result = layer_norm(hidden + feed_out, gain_ffn, shift_ffn)
    return result.reshape(seq_count, length, model_width)

def reference(tokens, seg_ids, pad_mask, w_query, w_key, w_value, w_out, w_in, w_back, b_query, b_value, b_out, gain_attn, shift_attn, b_in, b_back, gain_ffn, shift_ffn, conv_weight, cotangent):
    params = tuple((item.astype(jnp.float32) for item in (w_query, w_key, w_value, w_out, w_in, w_back, b_query, b_value, b_out, gain_attn, shift_attn, b_in, b_back, gain_ffn, shift_ffn, conv_weight)))
    group_size = 4
    seq_count = tokens.shape[0]
    group_count = seq_count // group_size
    token_groups = tokens.astype(jnp.float32).reshape(group_count, group_size, SEQ_LEN, D)
    cot_groups = cotangent.astype(jnp.float32).reshape(group_count, group_size, SEQ_LEN, D)
    seg_groups = seg_ids.reshape(group_count, group_size, SEQ_LEN)
    pad_groups = pad_mask.reshape(group_count, group_size, SEQ_LEN)

    def accumulate(carry, item):
        token_grp, seg_grp, pad_grp, cot_grp = item

        def local_layer(token_in, *weights):
            return block_forward(token_in, *weights, seg_grp, pad_grp)
        result, pullback = jax.vjp(local_layer, token_grp, *params)
        grads = pullback(cot_grp)
        carry = tuple((old + new for old, new in zip(carry, grads[1:])))
        return (carry, (result.astype(jnp.bfloat16), grads[0].astype(jnp.bfloat16)))
    start = tuple((jnp.zeros_like(item) for item in params))
    totals, (outputs, grad_rows) = lax.scan(accumulate, start, (token_groups, seg_groups, pad_groups, cot_groups))
    return (outputs.reshape(seq_count, SEQ_LEN, D), grad_rows.reshape(seq_count, SEQ_LEN, D), totals[0], totals[1], totals[2], totals[3], totals[4], totals[5], totals[6], totals[7], totals[8], totals[9], totals[10], totals[11], totals[12], totals[13], totals[14], totals[15])
```

```python
import functools

import jax
import jax.numpy as jnp
from jax import lax
from jax.experimental import pallas as pl
from jax.experimental.pallas import tpu as pltpu
from jax.sharding import PartitionSpec as P

BF, F32 = jnp.bfloat16, jnp.float32
VMEM_ALL = 67043328
norm_eps = 1e-05


def mm(a, b, dims=((1,), (0,))):
    return lax.dot_general(a, b, (dims, ((), ())), preferred_element_type=F32)


NT = ((1,), (1,))
TN = ((0,), (0,))


def moments(r):
    mean = jnp.mean(r, axis=-1, keepdims=True)
    cent = r - mean
    var = jnp.mean(cent * cent, axis=-1, keepdims=True)
    inv = lax.rsqrt(var + norm_eps)
    return cent * inv, inv


def norm_back(dn, n, inv):
    return (dn - jnp.mean(dn, axis=-1, keepdims=True) - n * jnp.mean(dn * n, axis=-1, keepdims=True)) * inv


def col_sum(v):
    return jnp.sum(v, axis=0, keepdims=True)


def ffn_kernel(x_ref, att_ref, cot_ref, key_ref, wo_ref, wi_ref, wb_ref, vec_ref, bi_ref,
               out_ref, do_ref, datt_ref, gwo_ref, gwi_ref, gwb_ref, gvec_ref, gbi_ref,
               act_s, gp_s, sum_s, hid_s, low_s, *, chunk):
    step = pl.program_id(0)
    inner = wi_ref.shape[1]
    chunks = inner // chunk

    @pl.when(step == 0)
    def _():
        for ref in (gwo_ref, gwi_ref, gwb_ref, gvec_ref, gbi_ref):
            ref[...] = jnp.zeros_like(ref)

    b_out, gain_a, shift_a = vec_ref[2:3, :], vec_ref[3:4, :], vec_ref[4:5, :]
    b_back, gain_f, shift_f = vec_ref[5:6, :], vec_ref[6:7, :], vec_ref[7:8, :]
    r1 = x_ref[...].astype(F32) + (mm(att_ref[...], wo_ref[...]) + b_out)
    n1, inv1 = moments(r1)
    hidden = n1 * gain_a + shift_a
    hid_s[...] = hidden
    low_s[...] = hidden.astype(BF)
    sum_s[...] = jnp.zeros_like(sum_s)

    def up(c, carry):
        cols = pl.ds(pl.multiple_of(c * chunk, chunk), chunk)
        u = mm(low_s[...], wi_ref[:, cols]) + bi_ref[:, cols]
        phi = 0.5 * (1.0 + lax.erf(u * 0.7071067811865476))
        act = (u * phi).astype(BF)
        gp_s[:, cols] = phi + u * (jnp.exp(u * u * -0.5) * 0.3989422804014327)
        act_s[:, cols] = act
        sum_s[...] += mm(act, wb_ref[cols, :])
        return carry

    lax.fori_loop(0, chunks, up, 0)
    n2, inv2 = moments(hid_s[...] + (sum_s[...] + b_back))
    out_ref[...] = (n2 * gain_f + shift_f).astype(BF)
    dy = cot_ref[...].astype(F32)
    gvec_ref[6:7, :] += col_sum(dy * n2)
    gvec_ref[7:8, :] += col_sum(dy)
    dr2 = norm_back(dy * gain_f, n2, inv2)
    df = dr2.astype(BF)
    gvec_ref[5:6, :] += col_sum(df.astype(F32))
    out2 = dr2
    sum_s[...] = out2
    do_ref[...] = df

    def down(c, carry):
        cols = pl.ds(pl.multiple_of(c * chunk, chunk), chunk)
        df = do_ref[...]
        du32 = mm(df, wb_ref[cols, :], NT) * gp_s[:, cols]
        du = du32.astype(BF)
        gwb_ref[cols, :] += mm(act_s[:, cols], df, TN)
        gbi_ref[:, cols] += col_sum(du.astype(F32))
        gwi_ref[:, cols] += mm(low_s[...], du, TN)
        sum_s[...] += mm(du, wi_ref[:, cols], NT)
        return carry

    lax.fori_loop(0, chunks, down, 0)
    dy1 = sum_s[...]
    r1 = x_ref[...].astype(F32) + (mm(att_ref[...], wo_ref[...]) + b_out)
    n1, inv1 = moments(r1)
    gvec_ref[3:4, :] += col_sum(dy1 * n1)
    gvec_ref[4:5, :] += col_sum(dy1)
    do = norm_back(dy1 * gain_a, n1, inv1).astype(BF)
    do_ref[...] = do
    gvec_ref[2:3, :] += col_sum(do.astype(F32))
    gwo_ref[...] += mm(att_ref[...], do, TN)
    live = (key_ref[...] >= 0).astype(F32)
    datt_ref[...] = (mm(do, wo_ref[...], NT) * live).astype(BF)


def ffn(x, att, cot, key_col, wo, wi, wb, vec, bi, tile=512, chunk=768):
    rows, d = x.shape
    inner = wi.shape[1]
    tile = min(tile, rows)
    row = pl.BlockSpec((tile, d), lambda i: (i, 0))
    one = lambda *s: pl.BlockSpec(s, lambda i: tuple(0 for _ in s), pipeline_mode=pl.Buffered(1))
    return pl.pallas_call(
        functools.partial(ffn_kernel, chunk=chunk),
        grid=(rows // tile,),
        in_specs=[row, row, row, pl.BlockSpec((tile, 1), lambda i: (i, 0)), one(d, d), one(d, inner), one(inner, d), one(8, d), one(1, inner)],
        out_specs=[row, row, row, one(d, d), one(d, inner), one(inner, d), one(8, d), one(1, inner)],
        out_shape=[jax.ShapeDtypeStruct((rows, d), BF)] * 3 + [
            jax.ShapeDtypeStruct((d, d), F32), jax.ShapeDtypeStruct((d, inner), F32), jax.ShapeDtypeStruct((inner, d), F32),
            jax.ShapeDtypeStruct((8, d), F32), jax.ShapeDtypeStruct((1, inner), F32)],
        scratch_shapes=[pltpu.VMEM((tile, inner), BF), pltpu.VMEM((tile, inner), F32), pltpu.VMEM((tile, d), F32), pltpu.VMEM((tile, d), F32), pltpu.VMEM((tile, d), BF)],
        compiler_params=pltpu.CompilerParams(vmem_limit_bytes=VMEM_ALL),
        name="ffn",
    )(x, att, cot, key_col, wo, wi, wb, vec, bi)


NEG = -1e30
GW = 256
BLK = 128
WIN = 256


def spread(w, mask):
    return jnp.concatenate([w] * 4, axis=0) * mask


def fold(b, mask):
    b = b * mask
    n = b.shape[0] // 4
    return (b[0:n] + b[n:2 * n]) + (b[2 * n:3 * n] + b[3 * n:4 * n])


def split(w):
    hi = w.astype(BF)
    return hi, (w - hi.astype(F32)).astype(BF)


def dot3(left, right, mask):
    lh, ll = left
    rh, rl = right
    n = lh.shape[0]
    two = mm(jnp.concatenate([lh, ll], axis=0), spread(rh, mask))
    return two[:n] + (two[n:] + mm(lh, spread(rl, mask)))


def head_swap(w):
    t = w.T
    n = w.shape[0]
    parts = [t[h * n:(h + 1) * n, :] for h in range(4)]
    return jnp.concatenate(parts, axis=1)


def lane_group(shape):
    return lax.broadcasted_iota(jnp.int32, shape, 1) // 64


def attn_fwd_kernel(x_ref, wq_ref, wk_ref, wv_ref, vec_ref, keyc_ref, keyr_ref, kwin_ref, lkc_ref, lkr_ref, cw_ref,
                    q_ref, k_ref, v_ref, lq_ref, lk_ref, fm_ref, bm_ref, at_ref, aw_ref, fro_ref,
                    zs_ref, ps_ref, b2_ref, b3_ref, zf_ref, sw_ref, g_ref, att_ref,
                    sc_s, cv_s, tap_s, z_s, *, seqs, length, land, taps):
    d = x_ref.shape[1]
    groups = d // GW
    n = seqs * groups
    stride = length // land
    half = taps // 2
    heads = d // 64
    scale = 0.125
    mask32 = (lax.broadcasted_iota(jnp.int32, (GW, GW), 0) // 64 == lax.broadcasted_iota(jnp.int32, (GW, GW), 1) // 64).astype(F32)
    mask = mask32.astype(BF)
    eye = (lax.broadcasted_iota(jnp.int32, (64, GW), 0) == lax.broadcasted_iota(jnp.int32, (64, GW), 1) % 64).astype(F32)

    def project(b, carry):
        rows = pl.ds(pl.multiple_of(b * length, length), length)
        xb = x_ref[rows, :]
        q_ref[rows, :] = (mm(xb, wq_ref[...]) + vec_ref[0:1, :]).astype(BF)
        k_ref[rows, :] = mm(xb, wk_ref[...]).astype(BF)
        v_ref[b, 0:half, :] = jnp.zeros((half, d), BF)
        v_ref[b, length + half:, :] = jnp.zeros((v_ref.shape[1] - length - half, d), BF)
        v_ref[b, half:half + length, :] = (mm(xb, wv_ref[...]) + vec_ref[1:2, :]).astype(BF)
        lrows = pl.ds(pl.multiple_of(b * land, land), land)
        member = ((lax.broadcasted_iota(jnp.int32, (land, length), 1) // stride == lax.broadcasted_iota(jnp.int32, (land, length), 0))
                  & (lkc_ref[lrows, :] == keyr_ref[b])).astype(F32)
        count = jnp.maximum(jnp.sum(member, axis=1, keepdims=True), 1.0)
        memb = member.astype(BF)
        lq_ref[lrows, :] = (mm(memb, q_ref[rows, :]) / count).astype(BF)
        lk_ref[lrows, :] = (mm(memb, k_ref[rows, :]) / count).astype(BF)
        return carry

    lax.fori_loop(0, seqs, project, 0)

    for h in range(heads):
        tap_s[h * BLK:(h + 1) * BLK, :] = pltpu.roll(
            jnp.broadcast_to(cw_ref[h:h + 1, :], (BLK, WIN)), 0, 1, stride=1, stride_axis=0).astype(BF)

    def scores(i, carry):
        b, g = i // groups, i % groups
        rows = pl.ds(pl.multiple_of(b * length, length), length)
        lrows = pl.ds(pl.multiple_of(b * land, land), land)
        cols = pl.ds(pl.multiple_of(g * GW, GW), GW)
        lq, lk = lq_ref[lrows, cols], lk_ref[lrows, cols]
        lqb, lkb = spread(lq, mask), spread(lk, mask)
        lkc, keyr = lkc_ref[lrows, :], keyr_ref[b]
        sc_s[...] = mm(lkb, q_ref[rows, cols], NT)
        half_l = length // 2
        for h in range(4):
            for t in range(2):
                tc = slice(t * half_l, (t + 1) * half_l)
                ok = lkc == keyr[:, tc]
                s = jnp.where(ok, sc_s[h * 64:(h + 1) * 64, tc] * scale, NEG)
                e = jnp.exp(s - jnp.max(s, axis=0, keepdims=True))
                fm_ref[i, h * 64:(h + 1) * 64, tc] = (e / jnp.sum(e, axis=0, keepdims=True)).astype(BF)
        sc_s[...] = mm(lqb, k_ref[rows, cols], NT)
        for h in range(4):
            for t in range(2):
                jr = slice(t * 32, (t + 1) * 32)
                ok = lkc[jr] == keyr
                s = jnp.where(ok, sc_s[h * 64 + t * 32:h * 64 + (t + 1) * 32, :] * scale, NEG)
                e = jnp.exp(s - jnp.max(s, axis=1, keepdims=True))
                live = (lkc[jr] >= 0).astype(F32)
                bm_ref[i, h * 64 + t * 32:h * 64 + (t + 1) * 32, :] = (e / jnp.sum(e, axis=1, keepdims=True) * live).astype(BF)
        vg = v_ref[b, half:half + length, cols]
        sw_ref[i] = fold(mm(bm_ref[i], vg), mask32)
        lkr = lkr_ref[b]
        s = jnp.where(lkc == lkr, mm(lk, lqb, NT) * scale, NEG)
        e = jnp.exp(s - jnp.max(s, axis=0, keepdims=True))
        at = e / jnp.sum(e, axis=0, keepdims=True) * (lkr >= 0).astype(F32)
        at_ref[i] = at
        aw_ref[i] = head_swap(at)
        cs = jnp.sum(at * at, axis=0, keepdims=True)
        lg = lane_group((1, GW))
        fro = jnp.zeros((1, GW), F32)
        for h in range(4):
            fro += jnp.where(lg == h, jnp.sum(jnp.where(lg == h, cs, 0.0), axis=1, keepdims=True), 0.0)
        fro = fro + 1e-6
        fro_ref[i] = fro
        z_s[i] = at / fro
        return carry

    lax.fori_loop(0, n, scores, 0)

    steps = zs_ref.shape[0]
    blocks = length // BLK
    per = -(-(seqs * blocks) // steps)

    def newton(step, carry):
        al, zl, pl_, b1, b2, b3 = ([None] * n for _ in range(6))
        for i in range(n):
            z = z_s[i]
            al[i], zl[i] = split(aw_ref[i]), split(z)
            zs_ref[step, i] = zl[i][0]
        for i in range(n):
            p = dot3(al[i], zl[i], mask)
            pl_[i] = split(p)
            ps_ref[step, i] = pl_[i][0]
            b1[i] = split(7.0 * eye - p)
        for i in range(n):
            v = 15.0 * eye - dot3(pl_[i], b1[i], mask)
            b2[i] = split(v)
            b2_ref[step, i] = b2[i][0]
        for i in range(n):
            v = 13.0 * eye - dot3(pl_[i], b2[i], mask)
            b3[i] = split(v)
            b3_ref[step, i] = b3[i][0]
        for i in range(n):
            z_s[i] = 0.25 * dot3(zl[i], b3[i], mask)

        def conv(m, c2):
            e = jnp.minimum(step * per + m, seqs * blocks - 1)
            b, blk = e // blocks, e % blocks
            trow = pl.ds(pl.multiple_of(e * BLK, BLK), BLK)
            kept = (keyc_ref[trow, :] == kwin_ref[e]).astype(F32).astype(BF)
            kept4 = jnp.concatenate([kept] * 4, axis=0)
            lg = lane_group((BLK, GW))
            for g in range(groups):
                band = tap_s[g * 4 * BLK:(g + 1) * 4 * BLK, :] * kept4
                y = mm(band, v_ref[b, pl.ds(pl.multiple_of(blk * BLK, BLK), WIN), g * GW:(g + 1) * GW])
                r = jnp.where(lg < 2, jnp.where(lg == 0, y[:BLK], y[BLK:2 * BLK]), jnp.where(lg == 2, y[2 * BLK:3 * BLK], y[3 * BLK:]))
                cv_s[trow, g * GW:(g + 1) * GW] = r
            return c2

        lax.fori_loop(0, per, conv, 0)
        return carry

    lax.fori_loop(0, steps, newton, 0)

    def finish(i, carry):
        b, g = i // groups, i % groups
        rows = pl.ds(pl.multiple_of(b * length, length), length)
        cols = pl.ds(pl.multiple_of(g * GW, GW), GW)
        z = z_s[i]
        zf_ref[i] = z
        gl = dot3(split(z), split(sw_ref[i]), mask).astype(BF)
        g_ref[i] = gl
        y = mm(fm_ref[i], spread(gl, mask), TN) + cv_s[rows, cols]
        att_ref[rows, cols] = jnp.where(keyc_ref[rows, :] >= 0, y, 0.0).astype(BF)
        return carry

    lax.fori_loop(0, n, finish, 0)


def vm(k):
    return [pl.BlockSpec(memory_space=pltpu.VMEM)] * k


def attn_fwd(x, wq, wk, wv, vec, keys, cw, seqs, land, taps, steps):
    keyc, keyr, kwin, lkc, lkr = keys
    rows, d = x.shape
    length = rows // seqs
    n = seqs * (d // GW)
    S = jax.ShapeDtypeStruct
    vrows = length - BLK + WIN
    outs = dict(
        q=S((rows, d), BF), k=S((rows, d), BF), v=S((seqs, vrows, d), BF), lq=S((seqs * land, d), BF), lk=S((seqs * land, d), BF),
        fm=S((n, GW, length), BF), bm=S((n, GW, length), BF), at=S((n, 64, GW), F32), aw=S((n, 64, GW), F32), fro=S((n, 1, GW), F32),
        zs=S((steps, n, 64, GW), BF), ps=S((steps, n, 64, GW), BF), b2=S((steps, n, 64, GW), BF), b3=S((steps, n, 64, GW), BF),
        zf=S((n, 64, GW), F32), sw=S((n, 64, GW), F32), g=S((n, 64, GW), BF), att=S((rows, d), BF))
    res = pl.pallas_call(
        functools.partial(attn_fwd_kernel, seqs=seqs, length=length, land=land, taps=taps),
        in_specs=vm(11), out_specs=vm(len(outs)), out_shape=list(outs.values()),
        scratch_shapes=[pltpu.VMEM((GW, length), F32), pltpu.VMEM((rows, d), F32), pltpu.VMEM((d // 64 * BLK, WIN), BF), pltpu.VMEM((n, 64, GW), F32)],
        compiler_params=pltpu.CompilerParams(vmem_limit_bytes=VMEM_ALL),
        name="attn_fwd",
    )(x, wq, wk, wv, vec, keyc, keyr, kwin, lkc, lkr, cw)
    return dict(zip(outs, res))


def make_keys(seg, pad, land, taps):
    seqs, length = seg.shape
    stride = length // land
    half = taps // 2
    live = pad == 1
    key = jnp.where(live, seg, -2)
    keyc = key.reshape(seqs * length, 1)
    keyr = key.reshape(seqs, 1, length)
    keyw = jnp.pad(jnp.where(live, seg, -1), ((0, 0), (half, WIN - BLK - half)), constant_values=-1)
    blocks = length // BLK
    kwin = jnp.stack([keyw[:, b * BLK:b * BLK + WIN] for b in range(blocks)], axis=1).reshape(seqs * blocks, 1, WIN)
    lead = jnp.where(live, seg, -1)[:, ::stride]
    lkc = lead.reshape(seqs * land, 1)
    lkr = jnp.tile(jnp.where(lead >= 0, lead, -3), (1, 4)).reshape(seqs, 1, 4 * land)
    return keyc, keyr, kwin, lkc, lkr


def make_taps(cw):
    heads, taps = cw.shape
    w = cw.astype(F32)
    return jnp.pad(w, ((0, 0), (0, WIN - taps))), jnp.pad(w[:, ::-1], ((0, 0), (0, WIN - taps)))


def attn_bwd_kernel(datt_ref, q_ref, k_ref, v_ref, lq_ref, lk_ref, fm_ref, bm_ref, at_ref, aw_ref, fro_ref,
                    zs_ref, ps_ref, b2_ref, b3_ref, zf_ref, sw_ref, g_ref,
                    keyc_ref, keyr_ref, kwin_ref, lkc_ref, cw_ref,
                    dq_ref, dk_ref, dv_ref, gc_ref,
                    sc_s, dp_s, tap_s, dsf_s, dsb_s, dv_s, d_s, da_s, dlq_s, dlk_s, x_s, *, seqs, length, land, taps):
    d = q_ref.shape[1]
    groups = d // GW
    n = seqs * groups
    stride = length // land
    half = taps // 2
    heads = d // 64
    scale = 0.125
    mask32 = (lax.broadcasted_iota(jnp.int32, (GW, GW), 0) // 64 == lax.broadcasted_iota(jnp.int32, (GW, GW), 1) // 64).astype(F32)
    mask = mask32.astype(BF)
    eye = (lax.broadcasted_iota(jnp.int32, (64, GW), 0) == lax.broadcasted_iota(jnp.int32, (64, GW), 1) % 64).astype(F32)

    for h in range(heads):
        tap_s[h * BLK:(h + 1) * BLK, :] = pltpu.roll(
            jnp.broadcast_to(cw_ref[h:h + 1, :], (BLK, WIN)), 0, 1, stride=1, stride_axis=0).astype(BF)
    for b in range(seqs):
        dp_s[b, 0:half, :] = jnp.zeros((half, d), BF)
        dp_s[b, half:half + length, :] = datt_ref[b * length:(b + 1) * length, :]
        dp_s[b, half + length:, :] = jnp.zeros((dp_s.shape[1] - length - half, d), BF)
    x_s[...] = jnp.zeros_like(x_s)

    def outer(i, carry):
        b, g = i // groups, i % groups
        rows = pl.ds(pl.multiple_of(b * length, length), length)
        cols = pl.ds(pl.multiple_of(g * GW, GW), GW)
        dg4 = datt_ref[rows, cols]
        sc_s[...] = mm(spread(g_ref[i], mask), dg4, NT)
        half_l = length // 2
        for h in range(4):
            for t in range(2):
                hr, tc = slice(h * 64, (h + 1) * 64), slice(t * half_l, (t + 1) * half_l)
                p, dp = fm_ref[i, hr, tc].astype(F32), sc_s[hr, tc]
                dsf_s[i, hr, tc] = (p * (dp - jnp.sum(dp * p, axis=0, keepdims=True))).astype(BF)
        gbd = mm(fm_ref[i], dg4) * mask32
        gh, gl = split(gbd)
        zh, zl = split(zf_ref[i])
        zh, zl = spread(zh, mask), spread(zl, mask)
        dsb = (mm(zh, gh, TN) + (mm(zl, gh, TN) + mm(zh, gl, TN))).astype(BF)
        d_s[i] = mm(sw_ref[i].astype(BF), gh, NT)
        da_s[i] = jnp.zeros((64, GW), F32)
        sc_s[...] = mm(dsb, v_ref[b, half:half + length, cols], NT)
        for h in range(8):
            hr = slice(h * 32, (h + 1) * 32)
            p, dp = bm_ref[i, hr, :].astype(F32), sc_s[hr, :]
            dsb_s[i, hr, :] = (p * (dp - jnp.sum(dp * p, axis=1, keepdims=True))).astype(BF)
        dv_s[rows, cols] = mm(bm_ref[i], dsb, TN)
        dlq_s[i] = fold(mm(dsb_s[i], k_ref[rows, cols]), mask32)
        dlk_s[i] = fold(mm(dsf_s[i], q_ref[rows, cols]), mask32)
        return carry

    lax.fori_loop(0, n, outer, 0)

    steps = zs_ref.shape[0]
    blocks = length // BLK
    per = -(-(seqs * blocks) // steps)

    def newton(r, carry):
        s = steps - 1 - r
        dl, db3, dp, db2, dz = ([None] * n for _ in range(5))
        for i in range(n):
            dl[i] = d_s[i].astype(BF)
        for i in range(n):
            db3[i] = (0.25 * mm(dl[i], spread(zs_ref[s, i], mask))).astype(BF)
            dz[i] = 0.25 * mm(b3_ref[s, i], spread(dl[i], mask))
        for i in range(n):
            dp[i] = mm(b2_ref[s, i], spread(db3[i], mask))
            db2[i] = (-mm(db3[i], spread(ps_ref[s, i], mask))).astype(BF)
        for i in range(n):
            p = ps_ref[s, i]
            b1 = (7.0 * eye - p.astype(F32)).astype(BF)
            dp[i] = dp[i] + mm(b1, spread(db2[i], mask)) - mm(db2[i], spread(p, mask))
            dp[i] = (-dp[i]).astype(BF)
        for i in range(n):
            da_s[i] += mm(zs_ref[s, i], spread(dp[i], mask))
            d_s[i] = dz[i] + mm(dp[i], spread(aw_ref[i].astype(BF), mask))

        def conv(m, c2):
            e = r * per + m

            @pl.when(e < seqs * blocks)
            def _():
                b, blk = e // blocks, e % blocks
                t0 = pl.multiple_of(blk * BLK, BLK)
                trow = pl.ds(pl.multiple_of(e * BLK, BLK), BLK)
                kept = (keyc_ref[trow, :] == kwin_ref[e]).astype(F32)
                kept4 = jnp.concatenate([kept.astype(BF)] * 4, axis=0)
                lg = lane_group((BLK, GW))
                for g in range(groups):
                    gc = slice(g * GW, (g + 1) * GW)
                    band = tap_s[g * 4 * BLK:(g + 1) * 4 * BLK, :] * kept4
                    y = mm(band, dp_s[b, pl.ds(t0, WIN), gc])
                    r4 = jnp.where(lg < 2, jnp.where(lg == 0, y[:BLK], y[BLK:2 * BLK]), jnp.where(lg == 2, y[2 * BLK:3 * BLK], y[3 * BLK:]))
                    dv_s[trow, gc] += r4
                    own = datt_ref[trow, gc]
                    four = jnp.concatenate([own * (lg == h).astype(F32).astype(BF) for h in range(4)], axis=0)
                    y = mm(four, v_ref[b, pl.ds(t0, WIN), gc], NT)
                    for h in range(4):
                        x_s[(g * 4 + h) * BLK:(g * 4 + h + 1) * BLK, :] += y[h * BLK:(h + 1) * BLK] * kept
            return c2

        lax.fori_loop(0, per, conv, 0)
        return carry

    lax.fori_loop(0, steps, newton, 0)

    ri = lax.broadcasted_iota(jnp.int32, (BLK, WIN), 0)
    for h in range(heads):
        v = x_s[h * BLK:(h + 1) * BLK, :]
        bit = 1
        while bit < BLK:
            v = jnp.where((ri & bit) != 0, pltpu.roll(v, WIN - bit, 1), v)
            bit *= 2
        gc_ref[h:h + 1, :] = jnp.sum(v, axis=0, keepdims=True)

    def finish(i, carry):
        b, g = i // groups, i % groups
        rows = pl.ds(pl.multiple_of(b * length, length), length)
        lrows = pl.ds(pl.multiple_of(b * land, land), land)
        cols = pl.ds(pl.multiple_of(g * GW, GW), GW)
        fro, at, aw, d0 = fro_ref[i], at_ref[i], aw_ref[i], d_s[i]
        cs = jnp.sum(d0 * aw, axis=0, keepdims=True)
        lg = lane_group((1, GW))
        tot = jnp.zeros((1, GW), F32)
        for h in range(4):
            tot += jnp.where(lg == h, jnp.sum(jnp.where(lg == h, cs, 0.0), axis=1, keepdims=True), 0.0)
        da = da_s[i] + head_swap(d0 / fro) - (2.0 * tot / (fro * fro)) * at
        dsa = (at * (da - jnp.sum(da * at, axis=0, keepdims=True))).astype(BF)
        lqb, lkb = spread(lq_ref[lrows, cols], mask), spread(lk_ref[lrows, cols], mask)
        member = ((lax.broadcasted_iota(jnp.int32, (land, length), 1) // stride == lax.broadcasted_iota(jnp.int32, (land, length), 0))
                  & (lkc_ref[lrows, :] == keyr_ref[b])).astype(F32)
        count = jnp.maximum(jnp.sum(member, axis=1, keepdims=True), 1.0)
        memb = member.astype(BF)
        dlk = (dlk_s[i] + mm(dsa, lqb)) * scale / count
        dlq = (dlq_s[i] + fold(mm(spread(dsa, mask), lkb, TN), mask32)) * scale / count
        yh, yl = split(dlq)
        dq_ref[rows, cols] = mm(jnp.concatenate([dsf_s[i], memb, memb], axis=0), jnp.concatenate([lkb * scale, yh, yl], axis=0), TN).astype(BF)
        yh, yl = split(dlk)
        dk_ref[rows, cols] = mm(jnp.concatenate([dsb_s[i], memb, memb], axis=0), jnp.concatenate([lqb * scale, yh, yl], axis=0), TN).astype(BF)
        dv_ref[rows, cols] = dv_s[rows, cols].astype(BF)
        return carry

    lax.fori_loop(0, n, finish, 0)


def attn_bwd(datt, sv, keys, cwb, seqs, land, taps):
    keyc, keyr, kwin, lkc, lkr = keys
    rows, d = datt.shape
    length = rows // seqs
    n = seqs * (d // GW)
    heads = d // 64
    S = jax.ShapeDtypeStruct
    V = pltpu.VMEM
    vrows = length - BLK + WIN
    names = ("q", "k", "v", "lq", "lk", "fm", "bm", "at", "aw", "fro", "zs", "ps", "b2", "b3", "zf", "sw", "g")
    return pl.pallas_call(
        functools.partial(attn_bwd_kernel, seqs=seqs, length=length, land=land, taps=taps),
        in_specs=vm(1 + len(names) + 5), out_specs=vm(4),
        out_shape=[S((rows, d), BF)] * 3 + [S((heads, WIN), F32)],
        scratch_shapes=[V((GW, length), F32), V((seqs, vrows, d), BF), V((heads * BLK, WIN), BF), V((n, GW, length), BF), V((n, GW, length), BF),
                        V((rows, d), F32)] + [V((n, 64, GW), F32)] * 4 + [V((heads * BLK, WIN), F32)],
        compiler_params=pltpu.CompilerParams(vmem_limit_bytes=VMEM_ALL),
        name="attn_bwd",
    )(datt, *[sv[k] for k in names], keyc, keyr, kwin, lkc, cwb)


def proj_kernel(x_ref, do_ref, dq_ref, dk_ref, dv_ref, wq_ref, wk_ref, wv_ref, gt_ref, gwq_ref, gwk_ref, gwv_ref, gb_ref):
    @pl.when(pl.program_id(0) == 0)
    def _():
        for ref in (gwq_ref, gwk_ref, gwv_ref, gb_ref):
            ref[...] = jnp.zeros_like(ref)

    x = x_ref[...]
    gwq_ref[...] += mm(x, dq_ref[...], TN)
    gwk_ref[...] += mm(x, dk_ref[...], TN)
    gwv_ref[...] += mm(x, dv_ref[...], TN)
    gb_ref[0:1, :] += col_sum(dq_ref[...].astype(F32))
    gb_ref[1:2, :] += col_sum(dv_ref[...].astype(F32))
    gt = do_ref[...].astype(F32) + mm(dq_ref[...], wq_ref[...], NT)
    gt = gt + mm(dk_ref[...], wk_ref[...], NT)
    gt_ref[...] = (gt + mm(dv_ref[...], wv_ref[...], NT)).astype(BF)


def proj_bwd(x, do, dq, dk, dv, wq, wk, wv, tile=1024):
    rows, d = x.shape
    tile = min(tile, rows)
    row = pl.BlockSpec((tile, d), lambda i: (i, 0))
    one = lambda *s: pl.BlockSpec(s, lambda i: tuple(0 for _ in s), pipeline_mode=pl.Buffered(1))
    S = jax.ShapeDtypeStruct
    return pl.pallas_call(
        proj_kernel, grid=(rows // tile,),
        in_specs=[row] * 5 + [one(d, d)] * 3,
        out_specs=[row] + [one(d, d)] * 3 + [one(8, d)],
        out_shape=[S((rows, d), BF)] + [S((d, d), F32)] * 3 + [S((8, d), F32)],
        compiler_params=pltpu.CompilerParams(vmem_limit_bytes=VMEM_ALL),
        name="proj_bwd",
    )(x, do, dq, dk, dv, wq, wk, wv)


AXES = ("dp", "fsdp")
LAND = 64
PINV_STEPS = 6


def per_device(tokens, seg_ids, pad_mask, w_query, w_key, w_value, w_out, w_in, w_back, b_query, b_value, b_out,
               gain_attn, shift_attn, b_in, b_back, gain_ffn, shift_ffn, conv_weight, cotangent):
    seqs, length, d = tokens.shape
    taps = conv_weight.shape[1]
    part = w_query.shape[0]
    inner = w_in.shape[1]
    small = jnp.concatenate([b_query, b_value, b_out, gain_attn, shift_attn, b_back, gain_ffn, shift_ffn, b_in])
    pad_rows = -(-small.shape[0] // d)
    small = jnp.pad(small, (0, pad_rows * d - small.shape[0])).reshape(pad_rows, d)
    first = lax.all_gather(jnp.concatenate([w_query, w_key, w_value, small], axis=0)[None], AXES, axis=0, tiled=True)
    ffw = jnp.concatenate([w_in[:, c * d:(c + 1) * d] for c in range(inner // d)], axis=0)
    second = lax.all_gather(jnp.concatenate([w_out, ffw, w_back], axis=0)[None], AXES, axis=0, tiled=True)
    n = first.shape[0]
    take = lambda s, k: s[:, k * part:(k + 1) * part].reshape(n * part, d)
    wq, wk, wv = (take(first, k) for k in range(3))
    small = first[:, 3 * part:].reshape(n, -1)
    vec = small[:, :8 * part].reshape(n, 8, part).transpose(1, 0, 2).reshape(8, n * part).astype(F32)
    bi = small[:, 8 * part:8 * part + inner // n].reshape(1, inner).astype(F32)
    wo = take(second, 0)
    wi = jnp.concatenate([take(second, 1 + c) for c in range(inner // d)], axis=1)
    wb = second[:, (1 + inner // d) * part:].reshape(inner, d)

    keys = make_keys(seg_ids, pad_mask, LAND, taps)
    taps_f, taps_b = make_taps(conv_weight)
    x = tokens.reshape(-1, d)
    sv = attn_fwd(x, wq, wk, wv, vec, keys, taps_f, seqs, LAND, taps, PINV_STEPS)
    out, do, datt, gwo, gwi, gwb, gvec, gbi = ffn(x, sv["att"], cotangent.reshape(-1, d), keys[0], wo, wi, wb, vec, bi, 512, 1024)
    split_rows = lambda g: g.astype(BF).reshape(n, -1, d)
    gi = jnp.concatenate([gwi[:, c * d:(c + 1) * d].astype(BF).reshape(n, part, d) for c in range(inner // d)], axis=1)
    late = lax.psum_scatter(jnp.concatenate([split_rows(gwo), gi, split_rows(gwb)], axis=1), AXES, scatter_dimension=0, tiled=True)[0].astype(F32)
    dq, dk, dv, gc = attn_bwd(datt, sv, keys, taps_b, seqs, LAND, taps)
    gt, gwq, gwk, gwv, gb = proj_bwd(x, do, dq, dk, dv, wq, wk, wv)
    last = lax.psum_scatter(jnp.concatenate([split_rows(gwq), split_rows(gwk), split_rows(gwv)], axis=1), AXES, scatter_dimension=0, tiled=True)[0].astype(F32)
    gvec = jnp.concatenate([gb[:2], gvec[2:]], axis=0)
    gvec, gbi, gc = lax.psum((gvec, gbi, gc), AXES)
    me = lax.axis_index(AXES)
    vs = lax.dynamic_slice(gvec, (0, me * part), (8, part))
    bs = lax.dynamic_slice(gbi[0], (me * (inner // n),), (inner // n,))
    go = late[:part]
    gi = jnp.concatenate([late[(1 + c) * part:(2 + c) * part] for c in range(inner // d)], axis=1)
    gbk = late[(1 + inner // d) * part:]
    return (out.reshape(tokens.shape), gt.reshape(tokens.shape), last[:part], last[part:2 * part], last[2 * part:], go, gi, gbk,
            vs[0], vs[1], vs[2], vs[3], vs[4], bs, vs[5], vs[6], vs[7], gc[:, :taps])


def solution(mesh):
    rows = P(AXES, None)
    seq = P(AXES, None, None)
    vector = P(AXES)
    in_specs = (seq, rows, rows) + (rows,) * 6 + (vector,) * 9 + (P(), seq)
    out_specs = (seq, seq) + (rows,) * 6 + (vector,) * 9 + (P(),)
    return jax.shard_map(per_device, mesh=mesh, in_specs=in_specs, out_specs=out_specs, check_vma=False)
```

```python
import functools

import jax
import jax.numpy as jnp
from jax import lax
from jax.experimental import pallas as pl
from jax.experimental.pallas import tpu as pltpu
from jax.sharding import PartitionSpec as P

BF, F32 = jnp.bfloat16, jnp.float32
VMEM_ALL = 67043328
norm_eps = 1e-05


def mm(a, b, dims=((1,), (0,))):
    return lax.dot_general(a, b, (dims, ((), ())), preferred_element_type=F32)


NT = ((1,), (1,))
TN = ((0,), (0,))


def moments(r):
    mean = jnp.mean(r, axis=-1, keepdims=True)
    cent = r - mean
    var = jnp.mean(cent * cent, axis=-1, keepdims=True)
    inv = lax.rsqrt(var + norm_eps)
    return cent * inv, inv


def norm_back(dn, n, inv):
    return (dn - jnp.mean(dn, axis=-1, keepdims=True) - n * jnp.mean(dn * n, axis=-1, keepdims=True)) * inv


def col_sum(v):
    return jnp.sum(v, axis=0, keepdims=True)


def ffn_kernel(x_ref, att_ref, cot_ref, key_ref, wo_ref, wi_ref, wb_ref, vec_ref, bi_ref,
               out_ref, do_ref, datt_ref, gwo_out, gwi_out, gwb_out, gvec_ref, gbi_ref,
               act_s, gp_s, sum_s, hid_s, low_s, gwo_ref, gwi_ref, gwb_ref, sems, *, chunk):
    step = pl.program_id(0)
    inner = wi_ref.shape[1]
    chunks = inner // chunk

    @pl.when(step == 0)
    def _():
        for ref in (gwo_ref, gwi_ref, gwb_ref, gvec_ref, gbi_ref):
            ref[...] = jnp.zeros_like(ref)

    b_out, gain_a, shift_a = vec_ref[2:3, :], vec_ref[3:4, :], vec_ref[4:5, :]
    b_back, gain_f, shift_f = vec_ref[5:6, :], vec_ref[6:7, :], vec_ref[7:8, :]
    r1 = x_ref[...].astype(F32) + (mm(att_ref[...], wo_ref[...]) + b_out)
    n1, inv1 = moments(r1)
    hidden = n1 * gain_a + shift_a
    hid_s[...] = hidden
    low_s[...] = hidden.astype(BF)
    sum_s[...] = jnp.zeros_like(sum_s)

    def up(c, carry):
        cols = pl.ds(pl.multiple_of(c * chunk, chunk), chunk)
        u = mm(low_s[...], wi_ref[:, cols]) + bi_ref[:, cols]
        phi = 0.5 * (1.0 + lax.erf(u * 0.7071067811865476))
        act = (u * phi).astype(BF)
        gp_s[:, cols] = phi + u * (jnp.exp(u * u * -0.5) * 0.3989422804014327)
        act_s[:, cols] = act
        sum_s[...] += mm(act, wb_ref[cols, :])
        return carry

    lax.fori_loop(0, chunks, up, 0)
    n2, inv2 = moments(hid_s[...] + (sum_s[...] + b_back))
    out_ref[...] = (n2 * gain_f + shift_f).astype(BF)
    dy = cot_ref[...].astype(F32)
    gvec_ref[6:7, :] += col_sum(dy * n2)
    gvec_ref[7:8, :] += col_sum(dy)
    dr2 = norm_back(dy * gain_f, n2, inv2)
    df = dr2.astype(BF)
    gvec_ref[5:6, :] += col_sum(df.astype(F32))
    out2 = dr2
    sum_s[...] = out2
    do_ref[...] = df

    def down(c, carry):
        cols = pl.ds(pl.multiple_of(c * chunk, chunk), chunk)
        df = do_ref[...]
        du32 = mm(df, wb_ref[cols, :], NT) * gp_s[:, cols]
        du = du32.astype(BF)
        gwb_ref[cols, :] += mm(act_s[:, cols], df, TN)
        gbi_ref[:, cols] += col_sum(du.astype(F32))
        gwi_ref[:, cols] += mm(low_s[...], du, TN)
        sum_s[...] += mm(du, wi_ref[:, cols], NT)
        return carry

    lax.fori_loop(0, chunks, down, 0)
    dy1 = sum_s[...]
    r1 = x_ref[...].astype(F32) + (mm(att_ref[...], wo_ref[...]) + b_out)
    n1, inv1 = moments(r1)
    gvec_ref[3:4, :] += col_sum(dy1 * n1)
    gvec_ref[4:5, :] += col_sum(dy1)
    do = norm_back(dy1 * gain_a, n1, inv1).astype(BF)
    do_ref[...] = do
    gvec_ref[2:3, :] += col_sum(do.astype(F32))
    gwo_ref[...] += mm(att_ref[...], do, TN)
    live = (key_ref[...] >= 0).astype(F32)
    datt_ref[...] = (mm(do, wo_ref[...], NT) * live).astype(BF)

    @pl.when(step == pl.num_programs(0) - 1)
    def _():
        d = gwo_ref.shape[0]
        fit = act_s.shape[0] // 2
        pieces = []
        for r in range(0, d, fit):
            pieces.append([(gwi_ref, gwi_out, r, inner, 0)])
        for src, dst in ((gwb_ref, gwb_out), (gwo_ref, gwo_out)):
            total = src.shape[0]
            for r in range(0, total, fit * (inner // d)):
                pieces.append([(src, dst, r + j * fit, d, j * d) for j in range(min(inner // d, (total - r) // fit))])
        flying = [None, None]
        for k, piece in enumerate(pieces):
            half = k % 2
            for c in flying[half] or ():
                c.wait()
            flying[half] = []
            for src, dst, r, width, col in piece:
                buf = act_s.at[pl.ds(half * fit, fit), pl.ds(col, width)]
                buf[...] = src[r:r + fit, :].astype(BF)
                flying[half].append(pltpu.make_async_copy(buf, dst.at[pl.ds(r, fit), :], sems.at[half, len(flying[half])]))
            for c in flying[half]:
                c.start()
        for cs in flying:
            for c in cs or ():
                c.wait()


def ffn(x, att, cot, key_col, wo, wi, wb, vec, bi, tile=512, chunk=768):
    rows, d = x.shape
    inner = wi.shape[1]
    tile = min(tile, rows)
    row = pl.BlockSpec((tile, d), lambda i: (i, 0))
    one = lambda *s: pl.BlockSpec(s, lambda i: tuple(0 for _ in s), pipeline_mode=pl.Buffered(1))
    return pl.pallas_call(
        functools.partial(ffn_kernel, chunk=chunk),
        grid=(rows // tile,),
        in_specs=[row, row, row, pl.BlockSpec((tile, 1), lambda i: (i, 0)), one(d, d), one(d, inner), one(inner, d), one(8, d), one(1, inner)],
        out_specs=[row, row, row] + [pl.BlockSpec(memory_space=pl.ANY)] * 3 + [one(8, d), one(1, inner)],
        out_shape=[jax.ShapeDtypeStruct((rows, d), BF)] * 3 + [
            jax.ShapeDtypeStruct((d, d), BF), jax.ShapeDtypeStruct((d, inner), BF), jax.ShapeDtypeStruct((inner, d), BF),
            jax.ShapeDtypeStruct((8, d), F32), jax.ShapeDtypeStruct((1, inner), F32)],
        scratch_shapes=[pltpu.VMEM((tile, inner), BF), pltpu.VMEM((tile, inner), F32), pltpu.VMEM((tile, d), F32), pltpu.VMEM((tile, d), F32), pltpu.VMEM((tile, d), BF), pltpu.VMEM((d, d), F32), pltpu.VMEM((d, inner), F32), pltpu.VMEM((inner, d), F32), pltpu.SemaphoreType.DMA((2, 4))],
        compiler_params=pltpu.CompilerParams(vmem_limit_bytes=VMEM_ALL),
        name="ffn",
    )(x, att, cot, key_col, wo, wi, wb, vec, bi)


NEG = -1e30
GW = 256
BLK = 128
WIN = 256


def spread(w, mask):
    return jnp.concatenate([w] * 4, axis=0) * mask


def fold(b, mask):
    b = b * mask
    n = b.shape[0] // 4
    return (b[0:n] + b[n:2 * n]) + (b[2 * n:3 * n] + b[3 * n:4 * n])


def split(w):
    hi = w.astype(BF)
    return hi, (w - hi.astype(F32)).astype(BF)


def dot3(left, right, mask):
    lh, ll = left
    rh, rl = right
    n = lh.shape[0]
    two = mm(jnp.concatenate([lh, ll], axis=0), spread(rh, mask))
    return two[:n] + (two[n:] + mm(lh, spread(rl, mask)))


def head_swap(w):
    t = w.T
    n = w.shape[0]
    parts = [t[h * n:(h + 1) * n, :] for h in range(4)]
    return jnp.concatenate(parts, axis=1)


def lane_group(shape):
    return lax.broadcasted_iota(jnp.int32, shape, 1) // 64


def attn_fwd_kernel(x_ref, wq_ref, wk_ref, wv_ref, vec_ref, keyc_ref, keyr_ref, kwin_ref, lkc_ref, lkr_ref, cw_ref,
                    q_ref, k_ref, v_ref, lq_ref, lk_ref, fm_ref, bm_ref, at_ref, aw_ref, fro_ref,
                    zs_ref, ps_ref, b2_ref, b3_ref, zf_ref, sw_ref, g_ref, att_ref,
                    sc_s, cv_s, tap_s, z_s, *, seqs, length, land, taps):
    d = x_ref.shape[1]
    groups = d // GW
    n = seqs * groups
    stride = length // land
    half = taps // 2
    heads = d // 64
    scale = 0.125
    mask32 = (lax.broadcasted_iota(jnp.int32, (GW, GW), 0) // 64 == lax.broadcasted_iota(jnp.int32, (GW, GW), 1) // 64).astype(F32)
    mask = mask32.astype(BF)
    eye = (lax.broadcasted_iota(jnp.int32, (64, GW), 0) == lax.broadcasted_iota(jnp.int32, (64, GW), 1) % 64).astype(F32)

    def project(b, carry):
        rows = pl.ds(pl.multiple_of(b * length, length), length)
        xb = x_ref[rows, :]
        q_ref[rows, :] = (mm(xb, wq_ref[...]) + vec_ref[0:1, :]).astype(BF)
        k_ref[rows, :] = mm(xb, wk_ref[...]).astype(BF)
        v_ref[b, 0:half, :] = jnp.zeros((half, d), BF)
        v_ref[b, length + half:, :] = jnp.zeros((v_ref.shape[1] - length - half, d), BF)
        v_ref[b, half:half + length, :] = (mm(xb, wv_ref[...]) + vec_ref[1:2, :]).astype(BF)
        lrows = pl.ds(pl.multiple_of(b * land, land), land)
        member = ((lax.broadcasted_iota(jnp.int32, (land, length), 1) // stride == lax.broadcasted_iota(jnp.int32, (land, length), 0))
                  & (lkc_ref[lrows, :] == keyr_ref[b])).astype(F32)
        count = jnp.maximum(jnp.sum(member, axis=1, keepdims=True), 1.0)
        memb = member.astype(BF)
        lq_ref[lrows, :] = (mm(memb, q_ref[rows, :]) / count).astype(BF)
        lk_ref[lrows, :] = (mm(memb, k_ref[rows, :]) / count).astype(BF)
        return carry

    lax.fori_loop(0, seqs, project, 0)

    for h in range(heads):
        tap_s[h * BLK:(h + 1) * BLK, :] = pltpu.roll(
            jnp.broadcast_to(cw_ref[h:h + 1, :], (BLK, WIN)), 0, 1, stride=1, stride_axis=0).astype(BF)

    def scores(i, carry):
        b, g = i // groups, i % groups
        rows = pl.ds(pl.multiple_of(b * length, length), length)
        lrows = pl.ds(pl.multiple_of(b * land, land), land)
        cols = pl.ds(pl.multiple_of(g * GW, GW), GW)
        lq, lk = lq_ref[lrows, cols], lk_ref[lrows, cols]
        lqb, lkb = spread(lq, mask), spread(lk, mask)
        lkc, keyr = lkc_ref[lrows, :], keyr_ref[b]
        sc_s[...] = mm(lkb, q_ref[rows, cols], NT)
        half_l = length // 2
        for h in range(4):
            for t in range(2):
                tc = slice(t * half_l, (t + 1) * half_l)
                ok = lkc == keyr[:, tc]
                s = jnp.where(ok, sc_s[h * 64:(h + 1) * 64, tc] * scale, NEG)
                e = jnp.exp(s - jnp.max(s, axis=0, keepdims=True))
                fm_ref[i, h * 64:(h + 1) * 64, tc] = (e / jnp.sum(e, axis=0, keepdims=True)).astype(BF)
        sc_s[...] = mm(lqb, k_ref[rows, cols], NT)
        for h in range(4):
            for t in range(2):
                jr = slice(t * 32, (t + 1) * 32)
                ok = lkc[jr] == keyr
                s = jnp.where(ok, sc_s[h * 64 + t * 32:h * 64 + (t + 1) * 32, :] * scale, NEG)
                e = jnp.exp(s - jnp.max(s, axis=1, keepdims=True))
                live = (lkc[jr] >= 0).astype(F32)
                bm_ref[i, h * 64 + t * 32:h * 64 + (t + 1) * 32, :] = (e / jnp.sum(e, axis=1, keepdims=True) * live).astype(BF)
        vg = v_ref[b, half:half + length, cols]
        sw_ref[i] = fold(mm(bm_ref[i], vg), mask32)
        lkr = lkr_ref[b]
        s = jnp.where(lkc == lkr, mm(lk, lqb, NT) * scale, NEG)
        e = jnp.exp(s - jnp.max(s, axis=0, keepdims=True))
        at = e / jnp.sum(e, axis=0, keepdims=True) * (lkr >= 0).astype(F32)
        at_ref[i] = at
        aw_ref[i] = head_swap(at)
        cs = jnp.sum(at * at, axis=0, keepdims=True)
        lg = lane_group((1, GW))
        fro = jnp.zeros((1, GW), F32)
        for h in range(4):
            fro += jnp.where(lg == h, jnp.sum(jnp.where(lg == h, cs, 0.0), axis=1, keepdims=True), 0.0)
        fro = fro + 1e-6
        fro_ref[i] = fro
        z_s[i] = at / fro
        return carry

    lax.fori_loop(0, n, scores, 0)

    steps = zs_ref.shape[0]
    blocks = length // BLK
    per = -(-(seqs * blocks) // steps)

    def newton(step, carry):
        al, zl, pl_, b1, b2, b3 = ([None] * n for _ in range(6))
        for i in range(n):
            z = z_s[i]
            al[i], zl[i] = split(aw_ref[i]), split(z)
            zs_ref[step, i] = zl[i][0]
        for i in range(n):
            p = dot3(al[i], zl[i], mask)
            pl_[i] = split(p)
            ps_ref[step, i] = pl_[i][0]
            b1[i] = split(7.0 * eye - p)
        for i in range(n):
            v = 15.0 * eye - dot3(pl_[i], b1[i], mask)
            b2[i] = split(v)
            b2_ref[step, i] = b2[i][0]
        for i in range(n):
            v = 13.0 * eye - dot3(pl_[i], b2[i], mask)
            b3[i] = split(v)
            b3_ref[step, i] = b3[i][0]
        for i in range(n):
            z_s[i] = 0.25 * dot3(zl[i], b3[i], mask)

        def conv(m, c2):
            e = jnp.minimum(step * per + m, seqs * blocks - 1)
            b, blk = e // blocks, e % blocks
            trow = pl.ds(pl.multiple_of(e * BLK, BLK), BLK)
            kept = (keyc_ref[trow, :] == kwin_ref[e]).astype(F32).astype(BF)
            kept4 = jnp.concatenate([kept] * 4, axis=0)
            lg = lane_group((BLK, GW))
            for g in range(groups):
                band = tap_s[g * 4 * BLK:(g + 1) * 4 * BLK, :] * kept4
                y = mm(band, v_ref[b, pl.ds(pl.multiple_of(blk * BLK, BLK), WIN), g * GW:(g + 1) * GW])
                r = jnp.where(lg < 2, jnp.where(lg == 0, y[:BLK], y[BLK:2 * BLK]), jnp.where(lg == 2, y[2 * BLK:3 * BLK], y[3 * BLK:]))
                cv_s[trow, g * GW:(g + 1) * GW] = r
            return c2

        lax.fori_loop(0, per, conv, 0)
        return carry

    lax.fori_loop(0, steps, newton, 0)

    def finish(i, carry):
        b, g = i // groups, i % groups
        rows = pl.ds(pl.multiple_of(b * length, length), length)
        cols = pl.ds(pl.multiple_of(g * GW, GW), GW)
        z = z_s[i]
        zf_ref[i] = z
        gl = dot3(split(z), split(sw_ref[i]), mask).astype(BF)
        g_ref[i] = gl
        y = mm(fm_ref[i], spread(gl, mask), TN) + cv_s[rows, cols]
        att_ref[rows, cols] = jnp.where(keyc_ref[rows, :] >= 0, y, 0.0).astype(BF)
        return carry

    lax.fori_loop(0, n, finish, 0)


def vm(k):
    return [pl.BlockSpec(memory_space=pltpu.VMEM)] * k


def attn_fwd(x, wq, wk, wv, vec, keys, cw, seqs, land, taps, steps):
    keyc, keyr, kwin, lkc, lkr = keys
    rows, d = x.shape
    length = rows // seqs
    n = seqs * (d // GW)
    S = jax.ShapeDtypeStruct
    vrows = length - BLK + WIN
    outs = dict(
        q=S((rows, d), BF), k=S((rows, d), BF), v=S((seqs, vrows, d), BF), lq=S((seqs * land, d), BF), lk=S((seqs * land, d), BF),
        fm=S((n, GW, length), BF), bm=S((n, GW, length), BF), at=S((n, 64, GW), F32), aw=S((n, 64, GW), F32), fro=S((n, 1, GW), F32),
        zs=S((steps, n, 64, GW), BF), ps=S((steps, n, 64, GW), BF), b2=S((steps, n, 64, GW), BF), b3=S((steps, n, 64, GW), BF),
        zf=S((n, 64, GW), F32), sw=S((n, 64, GW), F32), g=S((n, 64, GW), BF), att=S((rows, d), BF))
    res = pl.pallas_call(
        functools.partial(attn_fwd_kernel, seqs=seqs, length=length, land=land, taps=taps),
        in_specs=vm(11), out_specs=vm(len(outs)), out_shape=list(outs.values()),
        scratch_shapes=[pltpu.VMEM((GW, length), F32), pltpu.VMEM((rows, d), F32), pltpu.VMEM((d // 64 * BLK, WIN), BF), pltpu.VMEM((n, 64, GW), F32)],
        compiler_params=pltpu.CompilerParams(vmem_limit_bytes=VMEM_ALL),
        name="attn_fwd",
    )(x, wq, wk, wv, vec, keyc, keyr, kwin, lkc, lkr, cw)
    return dict(zip(outs, res))


def make_keys(seg, pad, land, taps):
    seqs, length = seg.shape
    stride = length // land
    half = taps // 2
    live = pad == 1
    key = jnp.where(live, seg, -2)
    keyc = key.reshape(seqs * length, 1)
    keyr = key.reshape(seqs, 1, length)
    keyw = jnp.pad(jnp.where(live, seg, -1), ((0, 0), (half, WIN - BLK - half)), constant_values=-1)
    blocks = length // BLK
    kwin = jnp.stack([keyw[:, b * BLK:b * BLK + WIN] for b in range(blocks)], axis=1).reshape(seqs * blocks, 1, WIN)
    lead = jnp.where(live, seg, -1)[:, ::stride]
    lkc = lead.reshape(seqs * land, 1)
    lkr = jnp.tile(jnp.where(lead >= 0, lead, -3), (1, 4)).reshape(seqs, 1, 4 * land)
    return keyc, keyr, kwin, lkc, lkr


def make_taps(cw):
    heads, taps = cw.shape
    w = cw.astype(F32)
    return jnp.pad(w, ((0, 0), (0, WIN - taps))), jnp.pad(w[:, ::-1], ((0, 0), (0, WIN - taps)))


def attn_bwd_kernel(datt_ref, q_ref, k_ref, v_ref, lq_ref, lk_ref, fm_ref, bm_ref, at_ref, aw_ref, fro_ref,
                    zs_ref, ps_ref, b2_ref, b3_ref, zf_ref, sw_ref, g_ref,
                    keyc_ref, keyr_ref, kwin_ref, lkc_ref, cw_ref,
                    dq_ref, dk_ref, dv_ref, gc_ref,
                    sc_s, dp_s, tap_s, dsf_s, dsb_s, dv_s, d_s, da_s, dlq_s, dlk_s, x_s, *, seqs, length, land, taps):
    d = q_ref.shape[1]
    groups = d // GW
    n = seqs * groups
    stride = length // land
    half = taps // 2
    heads = d // 64
    scale = 0.125
    mask32 = (lax.broadcasted_iota(jnp.int32, (GW, GW), 0) // 64 == lax.broadcasted_iota(jnp.int32, (GW, GW), 1) // 64).astype(F32)
    mask = mask32.astype(BF)
    eye = (lax.broadcasted_iota(jnp.int32, (64, GW), 0) == lax.broadcasted_iota(jnp.int32, (64, GW), 1) % 64).astype(F32)

    for h in range(heads):
        tap_s[h * BLK:(h + 1) * BLK, :] = pltpu.roll(
            jnp.broadcast_to(cw_ref[h:h + 1, :], (BLK, WIN)), 0, 1, stride=1, stride_axis=0).astype(BF)
    for b in range(seqs):
        dp_s[b, 0:half, :] = jnp.zeros((half, d), BF)
        dp_s[b, half:half + length, :] = datt_ref[b * length:(b + 1) * length, :]
        dp_s[b, half + length:, :] = jnp.zeros((dp_s.shape[1] - length - half, d), BF)
    x_s[...] = jnp.zeros_like(x_s)

    def outer(i, carry):
        b, g = i // groups, i % groups
        rows = pl.ds(pl.multiple_of(b * length, length), length)
        cols = pl.ds(pl.multiple_of(g * GW, GW), GW)
        dg4 = datt_ref[rows, cols]
        sc_s[...] = mm(spread(g_ref[i], mask), dg4, NT)
        half_l = length // 2
        for h in range(4):
            for t in range(2):
                hr, tc = slice(h * 64, (h + 1) * 64), slice(t * half_l, (t + 1) * half_l)
                p, dp = fm_ref[i, hr, tc].astype(F32), sc_s[hr, tc]
                dsf_s[i, hr, tc] = (p * (dp - jnp.sum(dp * p, axis=0, keepdims=True))).astype(BF)
        gbd = mm(fm_ref[i], dg4) * mask32
        gh, gl = split(gbd)
        zh, zl = split(zf_ref[i])
        zh, zl = spread(zh, mask), spread(zl, mask)
        dsb = (mm(zh, gh, TN) + (mm(zl, gh, TN) + mm(zh, gl, TN))).astype(BF)
        d_s[i] = mm(sw_ref[i].astype(BF), gh, NT)
        da_s[i] = jnp.zeros((64, GW), F32)
        sc_s[...] = mm(dsb, v_ref[b, half:half + length, cols], NT)
        for h in range(8):
            hr = slice(h * 32, (h + 1) * 32)
            p, dp = bm_ref[i, hr, :].astype(F32), sc_s[hr, :]
            dsb_s[i, hr, :] = (p * (dp - jnp.sum(dp * p, axis=1, keepdims=True))).astype(BF)
        dv_s[rows, cols] = mm(bm_ref[i], dsb, TN)
        dlq_s[i] = fold(mm(dsb_s[i], k_ref[rows, cols]), mask32)
        dlk_s[i] = fold(mm(dsf_s[i], q_ref[rows, cols]), mask32)
        return carry

    lax.fori_loop(0, n, outer, 0)

    steps = zs_ref.shape[0]
    blocks = length // BLK
    per = -(-(seqs * blocks) // steps)

    def newton(r, carry):
        s = steps - 1 - r
        dl, db3, dp, db2, dz = ([None] * n for _ in range(5))
        for i in range(n):
            dl[i] = d_s[i].astype(BF)
        for i in range(n):
            db3[i] = (0.25 * mm(dl[i], spread(zs_ref[s, i], mask))).astype(BF)
            dz[i] = 0.25 * mm(b3_ref[s, i], spread(dl[i], mask))
        for i in range(n):
            dp[i] = mm(b2_ref[s, i], spread(db3[i], mask))
            db2[i] = (-mm(db3[i], spread(ps_ref[s, i], mask))).astype(BF)
        for i in range(n):
            p = ps_ref[s, i]
            b1 = (7.0 * eye - p.astype(F32)).astype(BF)
            dp[i] = dp[i] + mm(b1, spread(db2[i], mask)) - mm(db2[i], spread(p, mask))
            dp[i] = (-dp[i]).astype(BF)
        for i in range(n):
            da_s[i] += mm(zs_ref[s, i], spread(dp[i], mask))
            d_s[i] = dz[i] + mm(dp[i], spread(aw_ref[i].astype(BF), mask))

        def conv(m, c2):
            e = r * per + m

            @pl.when(e < seqs * blocks)
            def _():
                b, blk = e // blocks, e % blocks
                t0 = pl.multiple_of(blk * BLK, BLK)
                trow = pl.ds(pl.multiple_of(e * BLK, BLK), BLK)
                kept = (keyc_ref[trow, :] == kwin_ref[e]).astype(F32)
                kept4 = jnp.concatenate([kept.astype(BF)] * 4, axis=0)
                lg = lane_group((BLK, GW))
                for g in range(groups):
                    gc = slice(g * GW, (g + 1) * GW)
                    band = tap_s[g * 4 * BLK:(g + 1) * 4 * BLK, :] * kept4
                    y = mm(band, dp_s[b, pl.ds(t0, WIN), gc])
                    r4 = jnp.where(lg < 2, jnp.where(lg == 0, y[:BLK], y[BLK:2 * BLK]), jnp.where(lg == 2, y[2 * BLK:3 * BLK], y[3 * BLK:]))
                    dv_s[trow, gc] += r4
                    own = datt_ref[trow, gc]
                    four = jnp.concatenate([own * (lg == h).astype(F32).astype(BF) for h in range(4)], axis=0)
                    y = mm(four, v_ref[b, pl.ds(t0, WIN), gc], NT)
                    for h in range(4):
                        x_s[(g * 4 + h) * BLK:(g * 4 + h + 1) * BLK, :] += y[h * BLK:(h + 1) * BLK] * kept
            return c2

        lax.fori_loop(0, per, conv, 0)
        return carry

    lax.fori_loop(0, steps, newton, 0)

    ri = lax.broadcasted_iota(jnp.int32, (BLK, WIN), 0)
    for h in range(heads):
        v = x_s[h * BLK:(h + 1) * BLK, :]
        bit = 1
        while bit < BLK:
            v = jnp.where((ri & bit) != 0, pltpu.roll(v, WIN - bit, 1), v)
            bit *= 2
        gc_ref[h:h + 1, :] = jnp.sum(v, axis=0, keepdims=True)

    def finish(i, carry):
        b, g = i // groups, i % groups
        rows = pl.ds(pl.multiple_of(b * length, length), length)
        lrows = pl.ds(pl.multiple_of(b * land, land), land)
        cols = pl.ds(pl.multiple_of(g * GW, GW), GW)
        fro, at, aw, d0 = fro_ref[i], at_ref[i], aw_ref[i], d_s[i]
        cs = jnp.sum(d0 * aw, axis=0, keepdims=True)
        lg = lane_group((1, GW))
        tot = jnp.zeros((1, GW), F32)
        for h in range(4):
            tot += jnp.where(lg == h, jnp.sum(jnp.where(lg == h, cs, 0.0), axis=1, keepdims=True), 0.0)
        da = da_s[i] + head_swap(d0 / fro) - (2.0 * tot / (fro * fro)) * at
        dsa = (at * (da - jnp.sum(da * at, axis=0, keepdims=True))).astype(BF)
        lqb, lkb = spread(lq_ref[lrows, cols], mask), spread(lk_ref[lrows, cols], mask)
        member = ((lax.broadcasted_iota(jnp.int32, (land, length), 1) // stride == lax.broadcasted_iota(jnp.int32, (land, length), 0))
                  & (lkc_ref[lrows, :] == keyr_ref[b])).astype(F32)
        count = jnp.maximum(jnp.sum(member, axis=1, keepdims=True), 1.0)
        memb = member.astype(BF)
        dlk = (dlk_s[i] + mm(dsa, lqb)) * scale / count
        dlq = (dlq_s[i] + fold(mm(spread(dsa, mask), lkb, TN), mask32)) * scale / count
        yh, yl = split(dlq)
        dq_ref[rows, cols] = mm(jnp.concatenate([dsf_s[i], memb, memb], axis=0), jnp.concatenate([lkb * scale, yh, yl], axis=0), TN).astype(BF)
        yh, yl = split(dlk)
        dk_ref[rows, cols] = mm(jnp.concatenate([dsb_s[i], memb, memb], axis=0), jnp.concatenate([lqb * scale, yh, yl], axis=0), TN).astype(BF)
        dv_ref[rows, cols] = dv_s[rows, cols].astype(BF)
        return carry

    lax.fori_loop(0, n, finish, 0)


def attn_bwd(datt, sv, keys, cwb, seqs, land, taps):
    keyc, keyr, kwin, lkc, lkr = keys
    rows, d = datt.shape
    length = rows // seqs
    n = seqs * (d // GW)
    heads = d // 64
    S = jax.ShapeDtypeStruct
    V = pltpu.VMEM
    vrows = length - BLK + WIN
    names = ("q", "k", "v", "lq", "lk", "fm", "bm", "at", "aw", "fro", "zs", "ps", "b2", "b3", "zf", "sw", "g")
    return pl.pallas_call(
        functools.partial(attn_bwd_kernel, seqs=seqs, length=length, land=land, taps=taps),
        in_specs=vm(1 + len(names) + 5), out_specs=vm(4),
        out_shape=[S((rows, d), BF)] * 3 + [S((heads, WIN), F32)],
        scratch_shapes=[V((GW, length), F32), V((seqs, vrows, d), BF), V((heads * BLK, WIN), BF), V((n, GW, length), BF), V((n, GW, length), BF),
                        V((rows, d), F32)] + [V((n, 64, GW), F32)] * 4 + [V((heads * BLK, WIN), F32)],
        compiler_params=pltpu.CompilerParams(vmem_limit_bytes=VMEM_ALL),
        name="attn_bwd",
    )(datt, *[sv[k] for k in names], keyc, keyr, kwin, lkc, cwb)


def proj_kernel(x_ref, do_ref, dq_ref, dk_ref, dv_ref, wq_ref, wk_ref, wv_ref, gt_ref, oq_ref, ok_ref, ov_ref, gb_ref, gwq_ref, gwk_ref, gwv_ref):
    @pl.when(pl.program_id(0) == 0)
    def _():
        for ref in (gwq_ref, gwk_ref, gwv_ref, gb_ref):
            ref[...] = jnp.zeros_like(ref)

    x = x_ref[...]
    gwq_ref[...] += mm(x, dq_ref[...], TN)
    gwk_ref[...] += mm(x, dk_ref[...], TN)
    gwv_ref[...] += mm(x, dv_ref[...], TN)
    gb_ref[0:1, :] += col_sum(dq_ref[...].astype(F32))
    gb_ref[1:2, :] += col_sum(dv_ref[...].astype(F32))
    gt = do_ref[...].astype(F32) + mm(dq_ref[...], wq_ref[...], NT)
    gt = gt + mm(dk_ref[...], wk_ref[...], NT)
    gt_ref[...] = (gt + mm(dv_ref[...], wv_ref[...], NT)).astype(BF)

    @pl.when(pl.program_id(0) == pl.num_programs(0) - 1)
    def _():
        for out, acc in ((oq_ref, gwq_ref), (ok_ref, gwk_ref), (ov_ref, gwv_ref)):
            out[...] = acc[...].astype(BF)


def proj_bwd(x, do, dq, dk, dv, wq, wk, wv, tile=1024):
    rows, d = x.shape
    tile = min(tile, rows)
    row = pl.BlockSpec((tile, d), lambda i: (i, 0))
    one = lambda *s: pl.BlockSpec(s, lambda i: tuple(0 for _ in s), pipeline_mode=pl.Buffered(1))
    S = jax.ShapeDtypeStruct
    return pl.pallas_call(
        proj_kernel, grid=(rows // tile,),
        in_specs=[row] * 5 + [one(d, d)] * 3,
        out_specs=[row] + [one(d, d)] * 3 + [one(8, d)],
        out_shape=[S((rows, d), BF)] + [S((d, d), BF)] * 3 + [S((8, d), F32)],
        scratch_shapes=[pltpu.VMEM((d, d), F32)] * 3,
        compiler_params=pltpu.CompilerParams(vmem_limit_bytes=VMEM_ALL),
        name="proj_bwd",
    )(x, do, dq, dk, dv, wq, wk, wv)

MESH = pl.DeviceIdType.MESH


class Place:
    def __init__(self, dp, fsdp):
        self.size = dict(z=dp // 2, y=2, x=fsdp // 2, c=2)
        i, j = lax.axis_index("dp"), lax.axis_index("fsdp")
        self.at = dict(z=i // 2, y=i % 2, x=j // 2, c=j % 2)

    def shift(self, axis, step):
        at = dict(self.at)
        at[axis] = lax.rem(at[axis] + step, self.size[axis])
        return at

    def device(self, at):
        return (at["z"] * 2 + at["y"], at["x"] * 2 + at["c"])

    def index(self, at):
        s = self.size
        return ((at["z"] * s["y"] + at["y"]) * s["x"] + at["x"]) * s["c"] + at["c"]

    def peers(self, axis):
        return [self.shift(axis, k) for k in range(1, self.size[axis])]

    def blocks(self, free, at):
        out = [dict(at)]
        for a in "zyxc":
            if a in free:
                out = [dict(o, **{a: v}) for o in out for v in range(self.size[a])]
        return out


def greet(place):
    barrier = pltpu.get_barrier_semaphore()
    count = 0
    for a in "zyxc":
        for at in place.peers(a):
            pl.semaphore_signal(barrier, inc=1, device_id=place.device(at), device_id_type=MESH)
            count += 1
    pl.semaphore_wait(barrier, count)


def send(src, dst, ssem, rsem, dev):
    return pltpu.make_async_remote_copy(src_ref=src, dst_ref=dst, send_sem=ssem, recv_sem=rsem, device_id=dev, device_id_type=MESH)


def units_of(part, d, parts):
    out = [(0, None), (1, None), (2, None), (3, None)]
    out += [(4, (slice(None), pl.ds(c * d, d))) for c in range(parts)]
    return out + [(5, (pl.ds(c * part, part), slice(None))) for c in range(parts)]


def unit_view(refs, unit, lead=None):
    a, cut = unit
    index = (() if lead is None else (lead,)) + (() if cut is None else cut)
    return refs[a].at[index] if index else refs[a]


class Gather:
    def __init__(self, place, own, to, units, orders, ssem, rsem, lsem):
        self.place, self.own, self.to, self.units, self.orders = place, own, to, units, orders
        self.ssem, self.rsem, self.lsem = ssem, rsem, lsem
        self.me = place.index(place.at)

    def copies(self, u, st):
        p, unit, order = self.place, self.units[u], self.orders[u]
        free, axis = order[:st], order[st]
        out = []
        for b in p.blocks(free, p.at):
            dst = unit_view(self.to, unit, p.index(b))
            src = unit_view(self.own, unit) if st == 0 else dst
            for at in p.peers(axis):
                out.append(send(src, dst, self.ssem.at[u, st], self.rsem.at[u, st], p.device(at)))
        return out

    def all_of(self, u, st):
        p, order = self.place, self.orders[u]
        count = (p.size[order[st]] - 1) * len(p.blocks(order[:st], p.at))
        ref = unit_view(self.to, self.units[u], pl.ds(0, count))
        return send(ref, ref, self.ssem.at[u, st], self.rsem.at[u, st], p.device(p.peers(order[st])[0]))

    def local(self, u):
        return pltpu.make_async_copy(unit_view(self.own, self.units[u]), unit_view(self.to, self.units[u], self.me), self.lsem.at[u])

    def start(self, us):
        for u in us:
            for c in self.copies(u, 0):
                c.start()
            self.local(u).start()

    def advance(self, u, st):
        self.all_of(u, st).wait_recv()
        if st == 0:
            self.local(u).wait()
        if st < 3:
            for c in self.copies(u, st + 1):
                c.start()

    def drain(self, us):
        for u in us:
            for st in range(4):
                self.all_of(u, st).wait_send()


def gather_kernel(q_ref, k_ref, v_ref, o_ref, i_ref, b_ref, s_ref, gq, gk, gv, go, gi, gb, gs, ssem, rsem, lsem, *, dp, fsdp):
    place = Place(dp, fsdp)
    greet(place)
    part, d = q_ref.shape
    units = units_of(part, d, i_ref.shape[1] // d) + [(6, None)]
    n = len(units)
    g = Gather(place, (q_ref, k_ref, v_ref, o_ref, i_ref, b_ref, s_ref), (gq, gk, gv, go, gi, gb, gs), units,
               [("zyxc", "zxyc")[u % 2] for u in range(n)], ssem, rsem, lsem)
    g.start(range(n))
    for st in range(4):
        for u in range(n):
            g.advance(u, st)
    g.drain(range(n))


def gather_all(shards, small, dp, fsdp):
    n = dp * fsdp
    part, d = shards[0].shape
    k = 4 + 2 * (shards[4].shape[1] // d) + 1
    arrays = tuple(shards) + (small,)
    D = pltpu.SemaphoreType.DMA
    return pl.pallas_call(
        functools.partial(gather_kernel, dp=dp, fsdp=fsdp),
        in_specs=vm(7), out_specs=[pl.BlockSpec(memory_space=pl.ANY)] * 7,
        out_shape=[jax.ShapeDtypeStruct((n,) + a.shape, a.dtype) for a in arrays],
        scratch_shapes=[D((k, 4)), D((k, 4)), D((k,))],
        compiler_params=pltpu.CompilerParams(collective_id=1, has_side_effects=True),
        name="gather",
    )(*arrays)


def reduce_kernel(gq, gk, gv, go, gi, gb, sm_ref, oq, ok, ov, oo, oi, ob, os_ref, r1, s1, r2, s2, r3, s3, r4, m_s, mr, ssem, rsem, msem, mrem, *, dp, fsdp):
    place = Place(dp, fsdp)
    greet(place)
    _, part, d = gq.shape
    parts = units_of(part, d, gi.shape[2] // d)
    units = len(parts)
    ins, outs = (gq, gk, gv, go, gi, gb), (oq, ok, ov, oo, oi, ob)
    here = place.at
    size = place.size

    def partial(u, at):
        return unit_view(ins, parts[u], place.index(at))

    orders = [("cxyz", "cyxz")[u % 2] for u in range(units)]

    def rank(at, axes):
        r = 0
        for a in axes:
            r = r * size[a] + at[a]
        return r

    def rest(u, st):
        return [a for a in "zyxc" if a not in orders[u][:st]]

    def outgoing(u, st, at):
        axis = orders[u][st - 1]
        base = dict(here)
        base[axis] = at[axis]
        return place.blocks(rest(u, st), base)

    recv = (None, r1, r2, r3, r4)
    sums = (None, s1, s2, s3)

    def stage_copies(u, st):
        axis = orders[u][st - 1]
        out = []
        for k in range(1, size[axis]):
            at = place.shift(axis, k)
            for b in outgoing(u, st, at):
                src = partial(u, b) if st == 1 else sums[st - 1].at[u, rank(b, rest(u, st - 1))]
                slot = rank(b, rest(u, st)) if st < 4 else k - 1
                out.append(send(src, recv[st].at[u, slot], ssem.at[u, st - 1], rsem.at[u, st - 1], place.device(at)))
        return out

    def all_of(u, st):
        whole = recv[st].at[u]
        return send(whole, whole, ssem.at[u, st - 1], rsem.at[u, st - 1], place.device(place.shift(orders[u][st - 1], 1)))

    def small_copies(st):
        axis = "cxyz"[st - 1]
        return [send(m_s.at[st - 1], mr.at[st - 1, k - 1], msem.at[st - 1, k - 1], mrem.at[st - 1, k - 1], place.device(place.shift(axis, k)))
                for k in range(1, size[axis])]

    m_s[0] = sm_ref[...]
    for u in range(units):
        for c in stage_copies(u, 1):
            c.start()
    small = small_copies(1)
    for c in small:
        c.start()
    for st in range(1, 5):
        for c in small:
            c.wait()
        total = m_s[st - 1]
        for k in range(len(small)):
            total = total + mr[st - 1, k]
        if st < 4:
            m_s[st] = total
            small = small_copies(st + 1)
            for c in small:
                c.start()
        else:
            os_ref[...] = total
        for u in range(units):
            all_of(u, st).wait_recv()
            if st < 4:
                for b in place.blocks(rest(u, st), here):
                    mine = partial(u, b)[...] if st == 1 else sums[st - 1][u, rank(b, rest(u, st - 1))]
                    slot = rank(b, rest(u, st))
                    sums[st][u, slot] = (mine.astype(F32) + recv[st][u, slot].astype(F32)).astype(BF)
                for c in stage_copies(u, st + 1):
                    c.start()
            else:
                t = s3[u, here["z"]].astype(F32)
                for k in range(size["z"] - 1):
                    t = t + r4[u, k].astype(F32)
                unit_view(outs, parts[u])[...] = t
    for u in range(units):
        for st in range(1, 5):
            all_of(u, st).wait_send()


def reduce_all(grads, sm, dp, fsdp):
    n, part, d = grads[0].shape
    k = 4 + 2 * (grads[4].shape[2] // d)
    S = jax.ShapeDtypeStruct
    V = pltpu.VMEM
    D = pltpu.SemaphoreType.DMA
    z, x = dp // 2, fsdp // 2
    blk = lambda m: V((k, m, part, d), BF)
    return pl.pallas_call(
        functools.partial(reduce_kernel, dp=dp, fsdp=fsdp),
        in_specs=vm(7), out_specs=vm(7),
        out_shape=[S(g.shape[1:], F32) for g in grads] + [S(sm.shape, F32)],
        scratch_shapes=[blk(z * 2 * x), blk(z * 2 * x), blk(z * 2), blk(z * 2), blk(z), blk(z), blk(z - 1),
                        V((4,) + sm.shape, F32), V((4, z - 1) + sm.shape, F32), D((k, 4)), D((k, 4)), D((4, z - 1)), D((4, z - 1))],
        compiler_params=pltpu.CompilerParams(collective_id=2, has_side_effects=True, vmem_limit_bytes=VMEM_ALL),
        name="reduce",
    )(*grads, sm)


AXES = ("dp", "fsdp")
LAND = 64
PINV_STEPS = 6


def per_device_native(tokens, seg_ids, pad_mask, w_query, w_key, w_value, w_out, w_in, w_back, b_query, b_value, b_out,
               gain_attn, shift_attn, b_in, b_back, gain_ffn, shift_ffn, conv_weight, cotangent):
    seqs, length, d = tokens.shape
    taps = conv_weight.shape[1]
    part = w_query.shape[0]
    inner = w_in.shape[1]
    small = jnp.concatenate([b_query, b_value, b_out, gain_attn, shift_attn, b_back, gain_ffn, shift_ffn, b_in])
    pad_rows = -(-small.shape[0] // d)
    small = jnp.pad(small, (0, pad_rows * d - small.shape[0])).reshape(pad_rows, d)
    first = lax.all_gather(jnp.concatenate([w_query, w_key, w_value, small], axis=0)[None], AXES, axis=0, tiled=True)
    ffw = jnp.concatenate([w_in[:, c * d:(c + 1) * d] for c in range(inner // d)], axis=0)
    second = lax.all_gather(jnp.concatenate([w_out, ffw, w_back], axis=0)[None], AXES, axis=0, tiled=True)
    n = first.shape[0]
    take = lambda s, k: s[:, k * part:(k + 1) * part].reshape(n * part, d)
    wq, wk, wv = (take(first, k) for k in range(3))
    small = first[:, 3 * part:].reshape(n, -1)
    vec = small[:, :8 * part].reshape(n, 8, part).transpose(1, 0, 2).reshape(8, n * part).astype(F32)
    bi = small[:, 8 * part:8 * part + inner // n].reshape(1, inner).astype(F32)
    wo = take(second, 0)
    wi = jnp.concatenate([take(second, 1 + c) for c in range(inner // d)], axis=1)
    wb = second[:, (1 + inner // d) * part:].reshape(inner, d)

    keys = make_keys(seg_ids, pad_mask, LAND, taps)
    taps_f, taps_b = make_taps(conv_weight)
    x = tokens.reshape(-1, d)
    sv = attn_fwd(x, wq, wk, wv, vec, keys, taps_f, seqs, LAND, taps, PINV_STEPS)
    out, do, datt, gwo, gwi, gwb, gvec, gbi = ffn(x, sv["att"], cotangent.reshape(-1, d), keys[0], wo, wi, wb, vec, bi, 512, 1024)
    split_rows = lambda g: g.reshape(n, -1, d)
    gi = jnp.concatenate([gwi[:, c * d:(c + 1) * d].reshape(n, part, d) for c in range(inner // d)], axis=1)
    late = lax.psum_scatter(jnp.concatenate([split_rows(gwo), gi, split_rows(gwb)], axis=1), AXES, scatter_dimension=0, tiled=True)[0].astype(F32)
    dq, dk, dv, gc = attn_bwd(datt, sv, keys, taps_b, seqs, LAND, taps)
    gt, gwq, gwk, gwv, gb = proj_bwd(x, do, dq, dk, dv, wq, wk, wv)
    last = lax.psum_scatter(jnp.concatenate([split_rows(gwq), split_rows(gwk), split_rows(gwv)], axis=1), AXES, scatter_dimension=0, tiled=True)[0].astype(F32)
    gvec = jnp.concatenate([gb[:2], gvec[2:]], axis=0)
    gvec, gbi, gc = lax.psum((gvec, gbi, gc), AXES)
    me = lax.axis_index(AXES)
    vs = lax.dynamic_slice(gvec, (0, me * part), (8, part))
    bs = lax.dynamic_slice(gbi[0], (me * (inner // n),), (inner // n,))
    go = late[:part]
    gi = jnp.concatenate([late[(1 + c) * part:(2 + c) * part] for c in range(inner // d)], axis=1)
    gbk = late[(1 + inner // d) * part:]
    return (out.reshape(tokens.shape), gt.reshape(tokens.shape), last[:part], last[part:2 * part], last[2 * part:], go, gi, gbk,
            vs[0], vs[1], vs[2], vs[3], vs[4], bs, vs[5], vs[6], vs[7], gc[:, :taps])


def per_device(dp, fsdp, *args):
    part = args[3].shape[0]
    if part % 8 or dp % 2 or fsdp % 2:
        return per_device_native(*args)
    (tokens, seg_ids, pad_mask, w_query, w_key, w_value, w_out, w_in, w_back, b_query, b_value, b_out,
     gain_attn, shift_attn, b_in, b_back, gain_ffn, shift_ffn, conv_weight, cotangent) = args
    seqs, length, d = tokens.shape
    taps = conv_weight.shape[1]
    inner = w_in.shape[1]
    n = dp * fsdp
    share = inner // n
    vecs = jnp.stack([b_query, b_value, b_out, gain_attn, shift_attn, b_back, gain_ffn, shift_ffn])
    small = jnp.pad(jnp.concatenate([vecs, b_in.reshape(8, share // 8)], axis=1).astype(F32), ((0, 0), (0, 128 - part - share // 8)))
    *weights, small = gather_all((w_query, w_key, w_value, w_out, w_in, w_back), small, dp, fsdp)
    wq, wk, wv, wo, wi, wb = (w.reshape(-1, w.shape[2]) for w in weights)
    vec = small[:, :, :part].transpose(1, 0, 2).reshape(8, d)
    bi = small[:, :, part:part + share // 8].reshape(1, inner)
    keys = make_keys(seg_ids, pad_mask, LAND, taps)
    taps_f, taps_b = make_taps(conv_weight)
    x = tokens.reshape(-1, d)
    sv = attn_fwd(x, wq, wk, wv, vec, keys, taps_f, seqs, LAND, taps, PINV_STEPS)
    out, do, datt, gwo, gwi, gwb, gvec, gbi = ffn(x, sv["att"], cotangent.reshape(-1, d), keys[0], wo, wi, wb, vec, bi, 512, 1024)
    dq, dk, dv, gc = attn_bwd(datt, sv, keys, taps_b, seqs, LAND, taps)
    gt, gwq, gwk, gwv, gb = proj_bwd(x, do, dq, dk, dv, wq, wk, wv)
    heads = gc.shape[0]
    pack = jnp.concatenate([gb[:2], gvec[2:], gbi.reshape(-1, d), gc[:, :d // heads].reshape(1, d)], axis=0)
    pack = jnp.pad(pack, ((0, -pack.shape[0] % 8), (0, 0)))
    *got, pack = reduce_all([g.reshape(n, -1, g.shape[1]) for g in (gwq, gwk, gwv, gwo, gwi, gwb)], pack, dp, fsdp)
    me = lax.axis_index(AXES)
    vs = lax.dynamic_slice(pack, (0, me * part), (8, part))
    bs = lax.dynamic_slice(pack[8:8 + inner // d].reshape(-1), (me * share,), (share,))
    gc = pack[8 + inner // d].reshape(heads, -1)[:, :taps]
    return (out.reshape(tokens.shape), gt.reshape(tokens.shape), *got,
            vs[0], vs[1], vs[2], vs[3], vs[4], bs, vs[5], vs[6], vs[7], gc)


def solution(mesh):
    rows = P(AXES, None)
    seq = P(AXES, None, None)
    vector = P(AXES)
    in_specs = (seq, rows, rows) + (rows,) * 6 + (vector,) * 9 + (P(), seq)
    out_specs = (seq, seq) + (rows,) * 6 + (vector,) * 9 + (P(),)
    return jax.shard_map(functools.partial(per_device, mesh.shape["dp"], mesh.shape["fsdp"]), mesh=mesh, in_specs=in_specs, out_specs=out_specs, check_vma=False)
```
